256 devices in a mesh: dp: 32 (over x, y, core), etp: 8 (over z).
Axes of the slice: x: 4, y: 4, z: 8, core: 2. Of those that a mesh axis runs over, the one named last changes fastest.
Arguments:
- tokens: bfloat16 [8192, 3072], P('dp'), may hold values from -6 to 6
- cotangent: bfloat16 [8192, 3072], P('dp'), may hold values from -6 to 6
- w_gate: float32 [2, 3072, 6144], P(None, 'dp', 'etp'), may hold values from -0.109375 to 0.109375
- w_up: float32 [2, 3072, 6144], P(None, 'dp', 'etp'), may hold values from -0.109375 to 0.109375
- w_down: float32 [2, 6144, 3072], P(None, 'etp', 'dp'), may hold values from -0.078125 to 0.078125
- slot_token: int32 [16384], P('dp'), may hold values from 0 to 255, as said below
- slot_gate: int32 [16384], P('dp'), may hold values from 0 to 16
- block_expert: int32 [128], P('dp'), may hold values from 0 to 2, as said below
Outputs:
- combined: bfloat16 [8192, 3072], P('dp', 'etp')
- input_grad: bfloat16 [8192, 3072], P('dp', 'etp')
The draws below stay inside these ranges and needn't reach their ends.
Inputs may be any that keep to these rules, and one draw needn't show every extreme that they name: `slot_token`: within the live blocks of one expert on one dp index no token repeats, so each expert has at most 2 live blocks there. `block_expert`: blocks of the experts and padding blocks stand in any order; each expert has at most 2 blocks on one dp index, and on some dp index every block is live.
All inputs are finite; a program needn't handle non-finite values.
Results may differ from the reference program's by a relative error of at most 0.014.
Values may be sent and summed in bfloat16 or wider, within the bound.
A program may use at most 128 MiB of HBM per device.

```python
import jax
import jax.numpy as jnp
from jax import lax

D = 3072
FF = 6144
E = 2
BLOCK = 128
TOK_DEV = 256
BLOCKS_DEV = 4
TOKENS = 8192
BLOCKS = 128
SLOTS = 16384
N_DP = 32
N_ETP = 8


def routing_tables(key):
    per_expert = TOK_DEV // BLOCK
    count_key, pick_key, order_key, token_key = jax.random.split(jax.random.fold_in(key, 7), 4)
    counts = jax.random.randint(count_key, (N_DP, 2), 0, per_expert + 1, dtype=jnp.int32)
    full_rank = jax.random.randint(pick_key, (), 0, N_DP, dtype=jnp.int32)
    rank_ids = jnp.arange(N_DP, dtype=jnp.int32)
    counts = jnp.where((rank_ids == full_rank)[:, None], per_expert, counts)
    positions = jnp.arange(BLOCKS_DEV, dtype=jnp.int32)[None, :]
    first = counts[:, :1]
    second = counts[:, 1:]
    labels = jnp.where(positions < first, 0, jnp.where(positions < first + second, 1, 2)).astype(jnp.int32)
    within = jnp.where(labels == 0, positions, jnp.where(labels == 1, positions - first, 0)).astype(jnp.int32)
    order_keys = jax.random.split(order_key, N_DP)
    orders = jax.vmap(lambda subkey: jax.random.permutation(subkey, BLOCKS_DEV))(order_keys).astype(jnp.int32)
    inverse = jnp.argsort(orders, axis=1, stable=True)
    block_labels = jnp.take_along_axis(labels, inverse, axis=1)
    block_within = jnp.take_along_axis(within, inverse, axis=1)
    token_keys = jax.random.split(token_key, N_DP * 2)
    shuffles = jax.vmap(lambda subkey: jax.random.permutation(subkey, TOK_DEV))(token_keys).astype(jnp.int32)
    shuffles = shuffles.reshape(N_DP, 2, per_expert, BLOCK)
    expert_pick = jnp.minimum(block_labels, 1)
    slot_tokens = shuffles[rank_ids[:, None], expert_pick, block_within]
    expert_ids = jnp.where(block_labels == 2, E, block_labels).astype(jnp.int32)
    return (slot_tokens.reshape(SLOTS).astype(jnp.int32), expert_ids.reshape(BLOCKS).astype(jnp.int32))


def draw_slot_token(key, part):
    return routing_tables(key)[0]


def draw_block_expert(key, part):
    return routing_tables(key)[1]


def place_ends(values, stream_key, least, top_value):
    longest = values.shape.index(max(values.shape))
    spots = []
    for shift in (0, 1):
        where = [jax.random.randint(jax.random.fold_in(stream_key, axis), (), 0, length) for axis, length in enumerate(values.shape)]
        where[longest] = (where[longest] + shift) % values.shape[longest]
        spots.append(tuple(where))
    return values.at[spots[0]].set(least).at[spots[1]].set(top_value)


def block_levels(key, shape, pieces, least, largest):
    level = 1.0
    for axis_at, shards_of in pieces:
        steps = jax.random.uniform(jax.random.fold_in(jax.random.fold_in(key, 6), axis_at), (shards_of,), jnp.float32, least / len(pieces), largest / len(pieces))
        level = level * jnp.repeat(jnp.exp(steps), shape[axis_at] // shards_of).reshape((-1,) + (1,) * (len(shape) - 1 - axis_at))
    return level


def normal_values(key, dims, width, bound, shards=(), kind=jnp.bfloat16):
    drawn = jax.random.normal(key, dims, jnp.float32) * width
    if len(shards) > 0:
        drawn = block_levels(key, dims, shards, -0.22, 0.18) * drawn
    return jnp.clip(drawn, min=-bound, max=bound).astype(kind)


def setup_inputs(seed: int = 0) -> dict:
    splits = jax.random.split(jax.random.key(seed), 9)
    return {
        "tokens": normal_values(splits[0], (TOKENS, D), 1.0, 6.0, ((0, 32),)),
        "cotangent": normal_values(splits[1], (TOKENS, D), 1.0, 6.0, ((0, 32),)),
        "w_gate": normal_values(splits[2], (E, D, FF), D ** -0.5, 0.109375, ((1, 32), (2, 8)), jnp.float32),
        "w_up": normal_values(splits[3], (E, D, FF), D ** -0.5, 0.109375, ((1, 32), (2, 8)), jnp.float32),
        "w_down": normal_values(splits[4], (E, FF, D), FF ** -0.5, 0.078125, ((1, 8), (2, 32)), jnp.float32),
        "slot_token": draw_slot_token(jax.random.fold_in(splits[8], 71), 0),
        "slot_gate": place_ends(jax.random.randint(splits[6], (SLOTS,), 0, 17), jax.random.fold_in(splits[6], 1), 0, 16).astype(jnp.int32),
        "block_expert": draw_block_expert(jax.random.fold_in(splits[8], 71), 0),
    }


gate_steps = 16.0


def reference(tokens, cotangent, w_gate, w_up, w_down, slot_token, slot_gate, block_expert):
    gate_low = w_gate.astype(jnp.bfloat16)
    up_low = w_up.astype(jnp.bfloat16)
    down_low = w_down.astype(jnp.bfloat16)
    experts_count = w_gate.shape[0]
    group_width = FF // N_ETP
    scale = slot_gate.astype(jnp.float32) / gate_steps

    def one_rank(rank_index):
        token_base = rank_index * TOK_DEV
        own_tokens = lax.dynamic_slice_in_dim(tokens, token_base, TOK_DEV, 0)
        own_cotangent = lax.dynamic_slice_in_dim(cotangent, token_base, TOK_DEV, 0)
        zeroed = jnp.zeros((N_ETP, TOK_DEV, D), jnp.float32)

        def step(totals, block_index):
            block_id = rank_index * BLOCKS_DEV + block_index
            expert = block_expert[block_id]

            def compute_block(state):
                y_total, dx_total = state
                chosen = jnp.minimum(expert, experts_count - 1)
                token_rows = lax.dynamic_slice_in_dim(slot_token, block_id * BLOCK, BLOCK, 0)
                gate_scale = lax.dynamic_slice_in_dim(scale, block_id * BLOCK, BLOCK, 0)[:, None]
                gate_mat = gate_low[chosen]
                up_mat = up_low[chosen]
                down_mat = down_low[chosen]
                inputs = own_tokens[token_rows]
                upstream = own_cotangent[token_rows]
                gate_pre = jnp.dot(inputs, gate_mat, preferred_element_type=jnp.float32)
                up_pre = jnp.dot(inputs, up_mat, preferred_element_type=jnp.float32)
                squash = jax.nn.sigmoid(gate_pre)
                active = gate_pre * squash
                hidden = (active * up_pre).astype(jnp.bfloat16)
                d_out = (gate_scale * upstream.astype(jnp.float32)).astype(jnp.bfloat16)
                d_hidden = jnp.dot(d_out, down_mat.T, preferred_element_type=jnp.float32)
                d_pre = (d_hidden * up_pre * squash * (1.0 + gate_pre * (1.0 - squash))).astype(jnp.bfloat16)
                d_up = (d_hidden * active).astype(jnp.bfloat16)
                produced_list = []
                backward_list = []
                for group in range(N_ETP):
                    columns = slice(group * group_width, (group + 1) * group_width)
                    produced = jnp.dot(hidden[:, columns], down_mat[columns], preferred_element_type=jnp.float32)
                    produced_list.append(produced * gate_scale)
                    backward = jnp.dot(d_pre[:, columns], gate_mat[:, columns].T, preferred_element_type=jnp.float32)
                    backward = backward + jnp.dot(d_up[:, columns], up_mat[:, columns].T, preferred_element_type=jnp.float32)
                    backward_list.append(backward)
                y_total = y_total.at[:, token_rows].add(jnp.stack(produced_list))
                dx_total = dx_total.at[:, token_rows].add(jnp.stack(backward_list))
                return y_total, dx_total

            def skip_block(state):
                return state

            return lax.cond(expert < experts_count, compute_block, skip_block, totals), None

        (y_total, dx_total), _ = lax.scan(step, (zeroed, zeroed), jnp.arange(BLOCKS_DEV, dtype=jnp.int32))
        y_low = lax.optimization_barrier(y_total.astype(jnp.bfloat16))
        dx_low = lax.optimization_barrier(dx_total.astype(jnp.bfloat16))
        combined_rows = jnp.sum(y_low.astype(jnp.float32), axis=0).astype(jnp.bfloat16)
        grad_rows = jnp.sum(dx_low.astype(jnp.float32), axis=0).astype(jnp.bfloat16)
        return combined_rows, grad_rows

    combined, input_grad = lax.map(one_rank, jnp.arange(N_DP, dtype=jnp.int32))
    return combined.reshape(TOKENS, D), input_grad.reshape(TOKENS, D)
```

```python
import functools

import jax
import jax.numpy as jnp
from jax import lax
from jax.experimental import pallas as pl
from jax.experimental.pallas import tpu as pltpu
from jax.sharding import PartitionSpec as P

MESH = pl.DeviceIdType.MESH
NX, NY, NC, NZ = 4, 4, 2, 8
ROWS = 96
HALF = ROWS // 2
D = NX * NY * NC * ROWS
F = 768
TOK = 256
COLS = D // NZ
PIECES = 6
KINDS = 12
NSUB = 2
SUB = TOK // 2 // NSUB
STEPS = NZ - 1
NT = (((1,), (1,)), ((), ()))
NN = (((1,), (0,)), ((), ()))
GATE, UP, DOWN = (0, 2), (1, 3), (4, 5)


def dot(a, b, dims):
    return lax.dot_general(a, b, dims, preferred_element_type=jnp.float32)


def kernel(
    expert_ref,
    slot_token_ref,
    slot_gate_ref,
    tokens_ref,
    cotangent_ref,
    w_gate_ref,
    w_up_ref,
    w_down_ref,
    y_ref,
    dx_ref,
    w_all,
    d_out,
    scale_ref,
    gate_pre,
    up_pre,
    d_hidden,
    hidden,
    d_pre,
    d_up,
    part,
    send_buf,
    recv_buf,
    g_send,
    g_recv,
    r_send,
    r_recv,
):
    dp = lax.axis_index("dp")
    z = lax.axis_index("etp")
    x, y, c = dp // 8, (dp // 2) % 4, dp % 2

    def dev(xx, yy, cc, zz):
        return ((xx % NX) * 8 + (yy % NY) * 2 + cc, zz % NZ)

    right, left = dev(x, y, c, z + 1), dev(x, y, c, z + NZ - 1)
    partner = dev(x, y, 1 - c, z)

    barrier = pltpu.get_barrier_semaphore()
    greeted = (
        dev(x + 1, y, c, z),
        dev(x + 3, y, c, z),
        dev(x, y + 1, c, z),
        dev(x, y + 3, c, z),
        partner,
        right,
        left,
    )
    for peer in greeted:
        pl.semaphore_signal(barrier, inc=1, device_id=peer, device_id_type=MESH)

    own = pl.multiple_of(c * ROWS, ROWS)
    other = pl.multiple_of((1 - c) * ROWS, ROWS)
    for e in range(2):
        w_all[GATE[e], x, y, pl.ds(own, ROWS), :] = w_gate_ref[e].astype(jnp.bfloat16)
        w_all[UP[e], x, y, pl.ds(own, ROWS), :] = w_up_ref[e].astype(jnp.bfloat16)
        w_all[DOWN[e], x, y, pl.ds(own, ROWS), :] = w_down_ref[e].astype(jnp.bfloat16)

    pl.semaphore_wait(barrier, len(greeted))

    def uv(p):
        return (x, y) if p % 2 == 0 else (y, x)

    def slot(p, u, v, start, size):
        u, v = u % 4, v % 4
        a, b = (u, v) if p % 2 == 0 else (v, u)
        return w_all.at[p, a, b, pl.ds(start, size), :]

    def line(p, v, start, size):
        v = v % 4
        if p % 2 == 0:
            return w_all.at[p, :, v, pl.ds(start, size), :]
        return w_all.at[p, v, :, pl.ds(start, size), :]

    def target(p, du, dv):
        return dev(x + du, y + dv, c, z) if p % 2 == 0 else dev(x + dv, y + du, c, z)

    def sent(p, k):
        u, v = uv(p)
        low, high = own, own + HALF
        if k < 4:
            step = 1 if k % 2 == 0 else 3
            if k < 2:
                ref = slot(p, u, v, own, ROWS)
            elif k == 2:
                ref = slot(p, u + 3, v, low, HALF)
            else:
                ref = slot(p, u + 1, v, high, HALF)
            return ref, target(p, step, 0)
        if k < 8:
            step = 1 if k % 2 == 0 else 3
            if k < 6:
                ref = line(p, v, own, ROWS)
            elif k == 6:
                ref = line(p, v + 3, low, HALF)
            else:
                ref = line(p, v + 1, high, HALF)
            return ref, target(p, 0, step)
        return line(p, v + (0, 3, 1, 2)[k - 8], own, ROWS), partner

    def landed(p, k):
        u, v = uv(p)
        low, high = own, own + HALF
        if k == 0:
            return slot(p, u + 3, v, own, ROWS)
        if k == 1:
            return slot(p, u + 1, v, own, ROWS)
        if k == 2:
            return slot(p, u + 2, v, low, HALF)
        if k == 3:
            return slot(p, u + 2, v, high, HALF)
        if k == 4:
            return line(p, v + 3, own, ROWS)
        if k == 5:
            return line(p, v + 1, own, ROWS)
        if k == 6:
            return line(p, v + 2, low, HALF)
        if k == 7:
            return line(p, v + 2, high, HALF)
        return line(p, v + (0, 3, 1, 2)[k - 8], other, ROWS)

    def copy(ref, peer, p, k):
        return pltpu.make_async_remote_copy(
            src_ref=ref,
            dst_ref=ref,
            send_sem=g_send.at[p, k],
            recv_sem=g_recv.at[p, k],
            device_id=peer,
            device_id_type=MESH,
        )

    def start(pair, *kinds):
        for k in kinds:
            for p in (2 * pair, 2 * pair + 1):
                ref, peer = sent(p, k)
                copy(ref, peer, p, k).start()

    def arrive(pair, *kinds):
        for k in kinds:
            for p in (2 * pair, 2 * pair + 1):
                copy(landed(p, k), partner, p, k).wait_recv()

    def forward_dot(lhs, p, out):
        @pl.loop(0, F // 256)
        def _(n):
            cols = pl.ds(pl.multiple_of(n * 256, 256), 256)
            rhs = w_all[p, :, :, :, cols].reshape(D, 256)
            out[:, cols] = dot(lhs[...], rhs, NN)

    def make_hidden(e):
        @pl.loop(0, TOK // 32)
        def _(i):
            rows = pl.ds(pl.multiple_of(i * 32, 32), 32)
            g = gate_pre[e, rows, :]
            squash = 1.0 / (1.0 + jnp.exp(-g))
            h = g * squash * up_pre[e, rows, :] * scale_ref[e, rows, :]
            hidden[e, rows, :] = h.astype(jnp.bfloat16)

    def make_d(e):
        @pl.loop(0, TOK // 32)
        def _(i):
            rows = pl.ds(pl.multiple_of(i * 32, 32), 32)
            g = gate_pre[e, rows, :]
            dh = d_hidden[e, rows, :]
            squash = 1.0 / (1.0 + jnp.exp(-g))
            dp_ = dh * up_pre[e, rows, :] * squash * (1.0 + g * (1.0 - squash))
            d_pre[e, rows, :] = dp_.astype(jnp.bfloat16)
            d_up[e, rows, :] = (dh * (g * squash)).astype(jnp.bfloat16)

    start(0, 0, 1)
    start(1, 0, 1)

    lane = lax.broadcasted_iota(jnp.int32, (1, 512), 1)
    block = [expert_ref[i] for i in range(4)]
    of_slot = jnp.where(
        lane < 128,
        block[0],
        jnp.where(lane < 256, block[1], jnp.where(lane < 384, block[2], block[3])),
    )
    amount = slot_gate_ref[...].astype(jnp.float32) / 16.0
    for e in range(2):
        amount_e = jnp.where(of_slot == e, amount, 0.0)

        @pl.loop(0, TOK // 64)
        def _(i):
            first = pl.multiple_of(i * 64, 64)
            token = lax.broadcasted_iota(jnp.int32, (64, 512), 0) + first
            hit = jnp.where(token == slot_token_ref[...], amount_e, 0.0)
            scale_ref[e, pl.ds(first, 64), :] = jnp.sum(hit, axis=1, keepdims=True)

    arrive(0, 0, 1)
    start(0, 2, 3)

    for e in range(2):

        @pl.loop(0, TOK // 16)
        def _(i):
            rows = pl.ds(pl.multiple_of(i * 16, 16), 16)
            up_rows = cotangent_ref[rows, :].astype(jnp.float32) * scale_ref[e, rows, :]
            d_out[e, rows, :] = up_rows.astype(jnp.bfloat16)

    arrive(0, 2, 3)
    start(0, 4, 5, 8)
    arrive(1, 0, 1)
    start(1, 2, 3)
    start(2, 0, 1)
    arrive(0, 4, 5)
    start(0, 6, 7, 9, 10)
    arrive(1, 2, 3)
    start(1, 4, 5, 8)
    arrive(2, 0, 1)
    start(2, 2, 3)
    arrive(0, 6, 7)
    start(0, 11)
    arrive(0, 8, 9, 10, 11)
    forward_dot(tokens_ref, GATE[0], gate_pre.at[0])
    forward_dot(tokens_ref, UP[0], up_pre.at[0])
    make_hidden(0)
    arrive(2, 2, 3)
    arrive(1, 4, 5)
    start(2, 4, 5, 8)
    start(1, 6, 7, 9, 10)
    arrive(1, 6, 7)
    start(1, 11)
    arrive(1, 8, 9, 10, 11)
    forward_dot(tokens_ref, GATE[1], gate_pre.at[1])
    arrive(2, 4, 5)
    start(2, 6, 7, 9, 10)
    forward_dot(tokens_ref, UP[1], up_pre.at[1])
    make_hidden(1)
    arrive(2, 6, 7)
    start(2, 11)
    arrive(2, 8, 9, 10, 11)

    def weight_block(p, b):
        rows = w_all[p, b // 2, pl.ds(2 * (b % 2), 2), :, :]
        return rows.reshape(COLS, F)

    def block_y(b):
        total = dot(hidden[0], weight_block(DOWN[0], b), NT)
        part[0, b] = total + dot(hidden[1], weight_block(DOWN[1], b), NT)

    def block_dx(b):
        total = dot(d_pre[0], weight_block(GATE[0], b), NT)
        total = total + dot(d_up[0], weight_block(UP[0], b), NT)
        total = total + dot(d_pre[1], weight_block(GATE[1], b), NT)
        part[1, b] = total + dot(d_up[1], weight_block(UP[1], b), NT)

    def compute(t, s):
        count = 2 if s < 3 else 1 if s < 5 else 0
        if count == 0:
            return

        @pl.loop(0, count)
        def _(i):
            if s == 4:
                b = z
            else:
                b = lax.rem(jnp.where(i == 0, z - 1 - s + NZ, z + 1 + s), NZ)
            if t == 0:
                block_y(b)
            else:
                block_dx(b)

    def hop(t, d, h, s):
        return pltpu.make_async_remote_copy(
            src_ref=send_buf.at[t, d, h, s],
            dst_ref=recv_buf.at[t, d, h, s],
            send_sem=r_send.at[t, d, h, s],
            recv_sem=r_recv.at[t, d, h, s],
            device_id=right if d == 0 else left,
            device_id_type=MESH,
        )

    def ring(t, s):
        compute(t, s)
        for h in range(NSUB):
            for d in range(2):
                b = lax.rem(z - 1 - s + NZ, NZ) if d == 0 else lax.rem(z + 1 + s, NZ)
                first = (d * NSUB + h) * SUB
                value = part[t, b, first : first + SUB, :]
                if s > 0:
                    hop(t, d, h, s - 1).wait_recv()
                    value = value + recv_buf[t, d, h, s - 1].astype(jnp.float32)
                send_buf[t, d, h, s] = value.astype(jnp.bfloat16)
                hop(t, d, h, s).start()

    def finish(t, out):
        for h in range(NSUB):
            for d in range(2):
                first = (d * NSUB + h) * SUB
                hop(t, d, h, STEPS - 1).wait_recv()
                value = part[t, z, first : first + SUB, :]
                value = value + recv_buf[t, d, h, STEPS - 1].astype(jnp.float32)
                out[first : first + SUB, :] = value.astype(jnp.bfloat16)

    ring(0, 0)
    forward_dot(d_out.at[0], DOWN[0], d_hidden.at[0])
    ring(0, 1)
    forward_dot(d_out.at[1], DOWN[1], d_hidden.at[1])
    ring(0, 2)
    make_d(0)
    make_d(1)
    ring(1, 0)
    for s in range(3, STEPS):
        ring(0, s)
        ring(1, s - 2)
    finish(0, y_ref)
    ring(1, STEPS - 2)
    ring(1, STEPS - 1)
    finish(1, dx_ref)

    for p in range(PIECES):
        for k in range(KINDS):
            copy(sent(p, k)[0], partner, p, k).wait_send()
    for t in range(2):
        for s in range(STEPS):
            for h in range(NSUB):
                for d in range(2):
                    hop(t, d, h, s).wait_send()


def shards(tokens, cotangent, w_gate, w_up, w_down, slot_token, slot_gate, block_expert):
    vmem = pl.BlockSpec(memory_space=pltpu.VMEM)
    smem = pl.BlockSpec(memory_space=pltpu.SMEM)
    wide = (2, TOK, F)
    ring_shape = (2, 2, NSUB, STEPS)
    out = jax.ShapeDtypeStruct((TOK, COLS), jnp.bfloat16)
    return pl.pallas_call(
        kernel,
        out_shape=(out, out),
        in_specs=[smem] + [vmem] * 7,
        out_specs=(vmem, vmem),
        scratch_shapes=[
            pltpu.VMEM((PIECES, NX, NY, NC * ROWS, F), jnp.bfloat16),
            pltpu.VMEM((2, TOK, D), jnp.bfloat16),
            pltpu.VMEM((2, TOK, 1), jnp.float32),
            pltpu.VMEM(wide, jnp.float32),
            pltpu.VMEM(wide, jnp.float32),
            pltpu.VMEM(wide, jnp.float32),
            pltpu.VMEM(wide, jnp.bfloat16),
            pltpu.VMEM(wide, jnp.bfloat16),
            pltpu.VMEM(wide, jnp.bfloat16),
            pltpu.VMEM((2, NZ, TOK, COLS), jnp.float32),
            pltpu.VMEM(ring_shape + (SUB, COLS), jnp.bfloat16),
            pltpu.VMEM(ring_shape + (SUB, COLS), jnp.bfloat16),
            pltpu.SemaphoreType.DMA((PIECES, KINDS)),
            pltpu.SemaphoreType.DMA((PIECES, KINDS)),
            pltpu.SemaphoreType.DMA(ring_shape),
            pltpu.SemaphoreType.DMA(ring_shape),
        ],
        compiler_params=pltpu.CompilerParams(
            collective_id=0, has_side_effects=True, vmem_limit_bytes=63 * 1024 * 1024
        ),
    )(
        block_expert,
        slot_token.reshape(1, -1),
        slot_gate.reshape(1, -1),
        tokens,
        cotangent,
        w_gate,
        w_up,
        jnp.swapaxes(w_down, 1, 2),
    )


def solution(mesh):
    in_specs = (
        P("dp", None),
        P("dp", None),
        P(None, "dp", "etp"),
        P(None, "dp", "etp"),
        P(None, "etp", "dp"),
        P("dp"),
        P("dp"),
        P("dp"),
    )
    out_specs = (P("dp", "etp"), P("dp", "etp"))
    return jax.shard_map(shards, mesh=mesh, in_specs=in_specs, out_specs=out_specs, check_vma=False)
```

```python
import functools

import jax
import jax.numpy as jnp
from jax import lax
from jax.experimental import pallas as pl
from jax.experimental.pallas import tpu as pltpu
from jax.sharding import PartitionSpec as P

MESH = pl.DeviceIdType.MESH
NX, NY, NC, NZ = 4, 4, 2, 8
ROWS = 96
HALF = ROWS // 2
D = NX * NY * NC * ROWS
F = 768
TOK = 256
COLS = D // NZ
PAIRS = (((0, 1), 0, ROWS), ((2, 3), 0, ROWS), ((4, 5), 0, ROWS))
KINDS = 19
NSUB = 2
SUB = TOK // 2 // NSUB
STEPS = NZ - 1
NT = (((1,), (1,)), ((), ()))
NN = (((1,), (0,)), ((), ()))
GATE, UP, DOWN = (0, 2), (1, 3), (4, 5)


def dot(a, b, dims):
    return lax.dot_general(a, b, dims, preferred_element_type=jnp.float32)


def kernel(
    expert_ref,
    slot_token_ref,
    slot_gate_ref,
    tokens_hbm,
    cotangent_hbm,
    w_gate_hbm,
    w_up_hbm,
    w_down_hbm,
    out_ref,
    tokens_ref,
    cotangent_ref,
    masters,
    w_all,
    d_out,
    scale_ref,
    gate_pre,
    up_pre,
    d_hidden,
    hidden,
    d_pre,
    d_up,
    part,
    send_buf,
    recv_buf,
    g_send,
    g_recv,
    r_send,
    r_recv,
    l_sem,
):
    dp = lax.axis_index("dp")
    z = lax.axis_index("etp")
    x, y, c = dp // 8, (dp // 2) % 4, dp % 2

    def dev(xx, yy, cc, zz):
        return ((xx % NX) * 8 + (yy % NY) * 2 + cc, zz % NZ)

    right, left = dev(x, y, c, z + 1), dev(x, y, c, z + NZ - 1)
    partner = dev(x, y, 1 - c, z)

    barrier = pltpu.get_barrier_semaphore()
    greeted = (
        dev(x + 1, y, c, z),
        dev(x + 3, y, c, z),
        dev(x, y + 1, c, z),
        dev(x, y + 3, c, z),
        partner,
        right,
        left,
    )
    for peer in greeted:
        pl.semaphore_signal(barrier, inc=1, device_id=peer, device_id_type=MESH)

    loads = [
        pltpu.make_async_copy(w_gate_hbm, masters.at[0], l_sem.at[0]),
        pltpu.make_async_copy(w_up_hbm, masters.at[1], l_sem.at[1]),
        pltpu.make_async_copy(w_down_hbm, masters.at[2], l_sem.at[2]),
        pltpu.make_async_copy(cotangent_hbm, cotangent_ref, l_sem.at[3]),
        pltpu.make_async_copy(tokens_hbm, tokens_ref, l_sem.at[4]),
    ]
    for load in loads:
        load.start()

    def cast(m, name, e):
        w_all[name[e], x, y, c, :, :] = masters[m, e].astype(jnp.bfloat16)

    def barrier_wait():
        pl.semaphore_wait(barrier, len(greeted))

    def place(pair, i, u, v, cc, first, size):
        m, r0, _ = PAIRS[pair]
        rows = pl.ds(r0 + first, size)
        if i == 0:
            return w_all.at[m[i], u, v, cc, rows, :]
        return w_all.at[m[i], v, u, cc, rows, :]

    def leg(pair, i, k):
        size = PAIRS[pair][2]
        half = size // 2
        u, v = (x, y) if i == 0 else (y, x)
        up = 1 if k % 2 == 0 else 3
        down = 4 - up

        def at(du, dv, first=0, count=size, cc=c):
            return place(pair, i, (u + du) % 4, (v + dv) % 4, cc, first, count)

        def line(part, dv, first=0, count=size, cc=c):
            uu = pl.ds(0, 4) if part is None else pl.ds(2 * part, 2)
            return place(pair, i, uu, (v + dv) % 4, cc, first, count)

        def peer(du, dv):
            return dev(x + du, y + dv, c, z) if i == 0 else dev(x + dv, y + du, c, z)

        if k < 2:
            return at(0, 0), peer(up, 0), at(down, 0)
        if k < 4:
            first = half * (k % 2)
            return at(down, 0, first, half), peer(up, 0), at(2, 0, first, half)
        if k < 8:
            part = (k - 4) // 2
            return line(part, 0), peer(0, up), line(part, down)
        if k < 12:
            part, first = (k - 8) // 2, half * (k % 2)
            return line(part, down, first, half), peer(0, up), line(part, 2, first, half)
        part, dv = ((None, 0), (0, 3), (0, 1), (1, 3), (1, 1), (0, 2), (1, 2))[k - 12]
        return line(part, dv), partner, line(part, dv, cc=1 - c)

    def copy(ref, peer, pair, i, k):
        return pltpu.make_async_remote_copy(
            src_ref=ref,
            dst_ref=ref,
            send_sem=g_send.at[2 * pair + i, k],
            recv_sem=g_recv.at[2 * pair + i, k],
            device_id=peer,
            device_id_type=MESH,
        )

    def start(pair, *kinds):
        for k in kinds:
            for i in range(2):
                ref, peer, _ = leg(pair, i, k)
                copy(ref, peer, pair, i, k).start()

    def arrive(pair, *kinds):
        for k in kinds:
            for i in range(2):
                copy(leg(pair, i, k)[2], partner, pair, i, k).wait_recv()

    def forward_dot(lhs, p, out):
        @pl.loop(0, F // 256)
        def _(n):
            cols = pl.ds(pl.multiple_of(n * 256, 256), 256)
            rhs = w_all[p, :, :, :, :, cols].reshape(D, 256)
            out[:, cols] = dot(lhs[...], rhs, NN)

    def make_hidden(e):
        @pl.loop(0, TOK // 32)
        def _(i):
            rows = pl.ds(pl.multiple_of(i * 32, 32), 32)
            g = gate_pre[e, rows, :]
            squash = 1.0 / (1.0 + jnp.exp(-g))
            h = g * squash * up_pre[e, rows, :] * scale_ref[e, rows, :]
            hidden[e, rows, :] = h.astype(jnp.bfloat16)

    def make_d(e):
        @pl.loop(0, TOK // 32)
        def _(i):
            rows = pl.ds(pl.multiple_of(i * 32, 32), 32)
            g = gate_pre[e, rows, :]
            dh = d_hidden[e, rows, :]
            squash = 1.0 / (1.0 + jnp.exp(-g))
            dp_ = dh * up_pre[e, rows, :] * squash * (1.0 + g * (1.0 - squash))
            d_pre[e, rows, :] = dp_.astype(jnp.bfloat16)
            d_up[e, rows, :] = (dh * (g * squash)).astype(jnp.bfloat16)

    loads[0].wait()
    cast(0, GATE, 0)
    loads[1].wait()
    cast(1, UP, 0)
    barrier_wait()
    start(0, 0, 1)
    cast(0, GATE, 1)
    cast(1, UP, 1)
    start(1, 0, 1)
    loads[2].wait()
    cast(2, DOWN, 0)
    cast(2, DOWN, 1)
    start(2, 0, 1)

    lane = lax.broadcasted_iota(jnp.int32, (1, 512), 1)
    block = [expert_ref[i] for i in range(4)]
    of_slot = jnp.where(
        lane < 128,
        block[0],
        jnp.where(lane < 256, block[1], jnp.where(lane < 384, block[2], block[3])),
    )
    amount = slot_gate_ref[...].astype(jnp.float32) / 16.0
    for e in range(2):
        amount_e = jnp.where(of_slot == e, amount, 0.0)

        @pl.loop(0, TOK // 64)
        def _(i):
            first = pl.multiple_of(i * 64, 64)
            token = lax.broadcasted_iota(jnp.int32, (64, 512), 0) + first
            hit = jnp.where(token == slot_token_ref[...], amount_e, 0.0)
            scale_ref[e, pl.ds(first, 64), :] = jnp.sum(hit, axis=1, keepdims=True)

    arrive(0, 0, 1)
    start(0, 2, 3)
    arrive(1, 0, 1)
    start(1, 2, 3)
    arrive(0, 2, 3)
    start(0, 4, 5, 6, 7, 12)
    arrive(2, 0, 1)
    start(2, 2, 3)
    arrive(1, 2, 3)
    loads[3].wait()
    for e in range(2):

        @pl.loop(0, TOK // 16)
        def _(i):
            rows = pl.ds(pl.multiple_of(i * 16, 16), 16)
            up_rows = cotangent_ref[rows, :].astype(jnp.float32) * scale_ref[e, rows, :]
            d_out[e, rows, :] = up_rows.astype(jnp.bfloat16)

    loads[4].wait()
    arrive(0, 4, 5)
    start(0, 8, 9, 13, 14)
    arrive(0, 6, 7)
    start(0, 10, 11, 15, 16)
    start(1, 4, 5, 6, 7, 12)
    arrive(2, 2, 3)
    arrive(0, 8, 9)
    start(0, 17)
    arrive(0, 10, 11)
    start(0, 18)
    arrive(0, 12, 13, 14, 15, 16, 17, 18)
    forward_dot(tokens_ref, GATE[0], gate_pre.at[0])
    forward_dot(tokens_ref, UP[0], up_pre.at[0])
    make_hidden(0)
    arrive(1, 4, 5)
    start(1, 8, 9, 13, 14)
    arrive(1, 6, 7)
    start(1, 10, 11, 15, 16)
    start(2, 4, 5, 6, 7, 12)
    arrive(1, 8, 9)
    start(1, 17)
    arrive(1, 10, 11)
    start(1, 18)
    arrive(1, 12, 13, 14, 15, 16, 17, 18)
    forward_dot(tokens_ref, GATE[1], gate_pre.at[1])
    forward_dot(tokens_ref, UP[1], up_pre.at[1])
    make_hidden(1)
    arrive(2, 4, 5)
    start(2, 8, 9, 13, 14)
    arrive(2, 6, 7)
    start(2, 10, 11, 15, 16)
    arrive(2, 8, 9)
    start(2, 17)
    arrive(2, 10, 11)
    start(2, 18)
    arrive(2, 12, 13, 14, 15, 16, 17, 18)

    def weight_block(p, b):
        rows = w_all[p, b // 2, pl.ds(2 * (b % 2), 2), :, :, :]
        return rows.reshape(COLS, F)

    def block_y(b):
        total = dot(hidden[0], weight_block(DOWN[0], b), NT)
        part[0, b] = total + dot(hidden[1], weight_block(DOWN[1], b), NT)

    def block_dx(b):
        total = dot(d_pre[0], weight_block(GATE[0], b), NT)
        total = total + dot(d_up[0], weight_block(UP[0], b), NT)
        total = total + dot(d_pre[1], weight_block(GATE[1], b), NT)
        part[1, b] = total + dot(d_up[1], weight_block(UP[1], b), NT)

    def compute(t, s):
        count = 2 if s < 3 else 1 if s < 5 else 0
        if count == 0:
            return

        @pl.loop(0, count)
        def _(i):
            if s == 4:
                b = z
            else:
                b = lax.rem(jnp.where(i == 0, z - 1 - s + NZ, z + 1 + s), NZ)
            if t == 0:
                block_y(b)
            else:
                block_dx(b)

    def hop(t, d, h, s):
        return pltpu.make_async_remote_copy(
            src_ref=send_buf.at[t, d, h, s],
            dst_ref=recv_buf.at[t, d, h, s],
            send_sem=r_send.at[t, d, h, s],
            recv_sem=r_recv.at[t, d, h, s],
            device_id=right if d == 0 else left,
            device_id_type=MESH,
        )

    def ring(t, s):
        compute(t, s)
        for h in range(NSUB):
            for d in range(2):
                b = lax.rem(z - 1 - s + NZ, NZ) if d == 0 else lax.rem(z + 1 + s, NZ)
                first = (d * NSUB + h) * SUB
                value = part[t, b, first : first + SUB, :]
                if s > 0:
                    hop(t, d, h, s - 1).wait_recv()
                    value = value + recv_buf[t, d, h, s - 1].astype(jnp.float32)
                send_buf[t, d, h, s] = value.astype(jnp.bfloat16)
                hop(t, d, h, s).start()

    def finish(t):
        for h in range(NSUB):
            for d in range(2):
                first = (d * NSUB + h) * SUB
                hop(t, d, h, STEPS - 1).wait_recv()
                value = part[t, z, first : first + SUB, :]
                value = value + recv_buf[t, d, h, STEPS - 1].astype(jnp.float32)
                out_ref[t, first : first + SUB, :] = value.astype(jnp.bfloat16)

    ring(0, 0)
    forward_dot(d_out.at[0], DOWN[0], d_hidden.at[0])
    ring(0, 1)
    forward_dot(d_out.at[1], DOWN[1], d_hidden.at[1])
    ring(0, 2)
    make_d(0)
    make_d(1)
    ring(1, 0)
    for s in range(3, STEPS):
        ring(0, s)
        ring(1, s - 2)
    finish(0)
    ring(1, STEPS - 2)
    ring(1, STEPS - 1)
    finish(1)

    for pair in range(len(PAIRS)):
        for i in range(2):
            for k in range(KINDS):
                copy(leg(pair, i, k)[0], partner, pair, i, k).wait_send()
    for t in range(2):
        for s in range(STEPS):
            for h in range(NSUB):
                for d in range(2):
                    hop(t, d, h, s).wait_send()


def shards(tokens, cotangent, w_gate, w_up, w_down, slot_token, slot_gate, block_expert):
    vmem = pl.BlockSpec(memory_space=pltpu.VMEM)
    smem = pl.BlockSpec(memory_space=pltpu.SMEM)
    wide = (2, TOK, F)
    ring_shape = (2, 2, NSUB, STEPS)
    hbm = pl.BlockSpec(memory_space=pl.ANY)
    sems = (2 * len(PAIRS), KINDS)
    out = pl.pallas_call(
        kernel,
        out_shape=jax.ShapeDtypeStruct((2, TOK, COLS), jnp.bfloat16),
        in_specs=[smem] + [vmem] * 2 + [hbm] * 5,
        out_specs=vmem,
        scratch_shapes=[
            pltpu.VMEM((TOK, D), jnp.bfloat16),
            pltpu.VMEM((TOK, D), jnp.bfloat16),
            pltpu.VMEM((3, 2, ROWS, F), jnp.float32),
            pltpu.VMEM((6, NX, NY, NC, ROWS, F), jnp.bfloat16),
            pltpu.VMEM((2, TOK, D), jnp.bfloat16),
            pltpu.VMEM((2, TOK, 1), jnp.float32),
            pltpu.VMEM(wide, jnp.float32),
            pltpu.VMEM(wide, jnp.float32),
            pltpu.VMEM(wide, jnp.float32),
            pltpu.VMEM(wide, jnp.bfloat16),
            pltpu.VMEM(wide, jnp.bfloat16),
            pltpu.VMEM(wide, jnp.bfloat16),
            pltpu.VMEM((2, NZ, TOK, COLS), jnp.float32),
            pltpu.VMEM(ring_shape + (SUB, COLS), jnp.bfloat16),
            pltpu.VMEM(ring_shape + (SUB, COLS), jnp.bfloat16),
            pltpu.SemaphoreType.DMA(sems),
            pltpu.SemaphoreType.DMA(sems),
            pltpu.SemaphoreType.DMA(ring_shape),
            pltpu.SemaphoreType.DMA(ring_shape),
            pltpu.SemaphoreType.DMA((5,)),
        ],
        compiler_params=pltpu.CompilerParams(
            collective_id=0, has_side_effects=True, vmem_limit_bytes=63 * 1024 * 1024
        ),
    )(
        block_expert,
        slot_token.reshape(1, -1),
        slot_gate.reshape(1, -1),
        tokens,
        cotangent,
        w_gate,
        w_up,
        jnp.swapaxes(w_down, 1, 2),
    )
    return out[0], out[1]


def solution(mesh):
    in_specs = (
        P("dp", None),
        P("dp", None),
        P(None, "dp", "etp"),
        P(None, "dp", "etp"),
        P(None, "etp", "dp"),
        P("dp"),
        P("dp"),
        P("dp"),
    )
    out_specs = (P("dp", "etp"), P("dp", "etp"))
    return jax.shard_map(shards, mesh=mesh, in_specs=in_specs, out_specs=out_specs, check_vma=False)
```

```python
import functools

import jax
import jax.numpy as jnp
from jax import lax
from jax.experimental import pallas as pl
from jax.experimental.pallas import tpu as pltpu
from jax.sharding import PartitionSpec as P

MESH = pl.DeviceIdType.MESH
NX, NY, NC, NZ = 4, 4, 2, 8
ROWS = 96
HALF = ROWS // 2
D = NX * NY * NC * ROWS
F = 768
TOK = 256
COLS = D // NZ
GROUPS = 3
GROUP = ROWS // GROUPS
GCOLS = COLS // GROUPS
GK = D // GROUPS
ALL, LOW, HIGH, OWN, NEAR, FAR = range(6)


def kinds_of(parts):
    kinds = [(name, ALL, sign) for name in ("near", "near2") for sign in (1, 3)]
    kinds += [(name, part, sign) for name in ("turn", "turn2") for part in parts for sign in (1, 3)]
    return kinds + [("core", ALL, step) for step in (0, 3, 1, 2)]


PAIRS = (
    ((0, 1), 0, ROWS, kinds_of((OWN, NEAR, FAR))),
    ((2, 3), 0, ROWS, kinds_of((LOW, HIGH))),
    ((4, 5), 0, GROUP, kinds_of((ALL,))),
    ((4, 5), GROUP, GROUP, kinds_of((ALL,))),
    ((4, 5), 2 * GROUP, GROUP, kinds_of((ALL,))),
)
FIRST = [2 * sum(len(pair[3]) for pair in PAIRS[:n]) for n in range(len(PAIRS) + 1)]
COPIES = FIRST[-1]
HOPS = NZ // 2
X_PARTS = 4
Y_PARTS = 2
NT = (((1,), (1,)), ((), ()))
NN = (((1,), (0,)), ((), ()))
GATE, UP, DOWN = (0, 2), (1, 3), (4, 5)


def dot(a, b, dims):
    return lax.dot_general(a, b, dims, preferred_element_type=jnp.float32)


def kernel(
    expert_ref,
    slot_token_hbm,
    slot_gate_hbm,
    tokens_hbm,
    cotangent_hbm,
    w_gate_hbm,
    w_up_hbm,
    w_down_hbm,
    out_ref,
    slot_token_ref,
    slot_gate_ref,
    tokens_ref,
    cotangent_ref,
    masters,
    w_all,
    perm,
    turned,
    d_out,
    scale_ref,
    pre,
    d_hidden,
    hidden,
    d_pre,
    d_up,
    part_y,
    part_x,
    y_rows,
    y_send,
    y_recv,
    x_send,
    x_recv,
    g_send,
    g_recv,
    ys_sem,
    yr_sem,
    xs_sem,
    xr_sem,
    l_sem,
):
    dp = lax.axis_index("dp")
    z = lax.axis_index("etp")
    x, y, c = dp // 8, (dp // 2) % 4, dp % 2

    def dev(xx, yy, cc, zz):
        return ((xx % NX) * 8 + (yy % NY) * 2 + cc, zz % NZ)

    right, left = dev(x, y, c, z + 1), dev(x, y, c, z + NZ - 1)
    partner = dev(x, y, 1 - c, z)

    barrier = pltpu.get_barrier_semaphore()
    greeted = (
        dev(x + 1, y, c, z),
        dev(x + 3, y, c, z),
        dev(x, y + 1, c, z),
        dev(x, y + 3, c, z),
        partner,
        right,
        left,
    )
    for peer in greeted:
        pl.semaphore_signal(barrier, inc=1, device_id=peer, device_id_type=MESH)

    loads = []
    for src, dst in (
        (w_gate_hbm.at[0], masters.at[0, 0]),
        (w_up_hbm.at[0], masters.at[1, 0]),
        (w_gate_hbm.at[1], masters.at[0, 1]),
        (w_up_hbm.at[1], masters.at[1, 1]),
        (w_down_hbm, masters.at[2]),
        (slot_token_hbm, slot_token_ref),
        (slot_gate_hbm, slot_gate_ref),
        (cotangent_hbm, cotangent_ref),
        (tokens_hbm, tokens_ref),
    ):
        loads.append(pltpu.make_async_copy(src, dst, l_sem.at[len(loads)]))
        loads[-1].start()

    def cast(m, name, e):
        w_all[name[e], x // 2, x % 2, y // 2, y % 2, c, :, :] = masters[m, e].astype(jnp.bfloat16)

    def barrier_wait():
        pl.semaphore_wait(barrier, len(greeted))

    whole = slice(None)

    def slot(u):
        return (u % 4) // 2, u % 2

    def leg(pair, i, kind):
        name, part, step = kind
        m, r0, size, _ = PAIRS[pair]
        half = size // 2
        u, v = (x, y) if i == 0 else (y, x)
        back = 4 - step
        first = half if step == 3 else 0
        us = {
            ALL: (whole, whole),
            LOW: (0, whole),
            HIGH: (1, whole),
            OWN: slot(u),
            NEAR: (whole, (u + 1) % 2),
            FAR: slot(u + 2),
        }[part]

        def at(uu, vv, start=0, count=size, cc=c):
            where = uu + vv if i == 0 else vv + uu
            return w_all.at[(m[i],) + where + (cc, pl.ds(r0 + start, count), whole)]

        def peer(du, dv):
            return dev(x + du, y + dv, c, z) if i == 0 else dev(x + dv, y + du, c, z)

        if name == "near":
            return at(slot(u), slot(v)), peer(step, 0), at(slot(u + back), slot(v))
        if name == "near2":
            mine = at(slot(u + back), slot(v), first, half)
            return mine, peer(step, 0), at(slot(u + 2), slot(v), first, half)
        if name == "turn":
            return at(us, slot(v)), peer(0, step), at(us, slot(v + back))
        if name == "turn2":
            mine = at(us, slot(v + back), first, half)
            return mine, peer(0, step), at(us, slot(v + 2), first, half)
        return at(us, slot(v + step)), partner, at(us, slot(v + step), cc=1 - c)

    def copy(ref, peer, pair, i, kind):
        kinds = PAIRS[pair][3]
        at = FIRST[pair] + i * len(kinds) + kinds.index(kind)
        return pltpu.make_async_remote_copy(
            src_ref=ref,
            dst_ref=ref,
            send_sem=g_send.at[at],
            recv_sem=g_recv.at[at],
            device_id=peer,
            device_id_type=MESH,
        )

    def start(pair, name, part=ALL, steps=(1, 3)):
        for step in steps:
            for i in range(2):
                ref, peer, _ = leg(pair, i, (name, part, step))
                copy(ref, peer, pair, i, (name, part, step)).start()

    def arrive(pair, name, part=ALL, steps=(1, 3)):
        for step in steps:
            for i in range(2):
                copy(leg(pair, i, (name, part, step))[2], partner, pair, i, (name, part, step)).wait_recv()

    def forward(first):
        @pl.loop(0, 2 * (F // 256))
        def _(j):
            m = first + j // (F // 256)
            cols = pl.ds(pl.multiple_of((j % (F // 256)) * 256, 256), 256)
            rhs = w_all[m, :, :, :, :, :, :, cols].reshape(D, 256)
            pre[m, :, cols] = dot(tokens_ref[...], rhs, NN)

    def add_d_hidden(g):
        @pl.loop(0, 2 * (F // 256))
        def _(j):
            e = j // (F // 256)
            cols = pl.ds(pl.multiple_of((j % (F // 256)) * 256, 256), 256)
            rhs = w_all[4 + e, :, :, :, :, :, pl.ds(g * GROUP, GROUP), cols].reshape(GK, 256)
            total = dot(d_out[e, g], rhs, NN)
            if g > 0:
                total = total + d_hidden[e, :, cols]
            d_hidden[e, :, cols] = total

    def make_hidden(e):
        @pl.loop(0, TOK // 32)
        def _(i):
            rows = pl.ds(pl.multiple_of(i * 32, 32), 32)
            gate = pre[2 * e, rows, :]
            squash = 1.0 / (1.0 + jnp.exp(-gate))
            h = gate * squash * pre[2 * e + 1, rows, :] * scale_ref[e, rows, :]
            hidden[e, rows, :] = h.astype(jnp.bfloat16)

    def make_d():
        @pl.loop(0, 2 * (TOK // 32))
        def _(j):
            e = j // (TOK // 32)
            rows = pl.ds(pl.multiple_of((j % (TOK // 32)) * 32, 32), 32)
            gate = pre[2 * e, rows, :]
            dh = d_hidden[e, rows, :]
            squash = 1.0 / (1.0 + jnp.exp(-gate))
            before = dh * pre[2 * e + 1, rows, :] * squash * (1.0 + gate * (1.0 - squash))
            d_pre[e, rows, :] = before.astype(jnp.bfloat16)
            d_up[e, rows, :] = (dh * (gate * squash)).astype(jnp.bfloat16)

    loads[0].wait()
    cast(0, GATE, 0)
    loads[1].wait()
    cast(1, UP, 0)
    barrier_wait()
    start(0, "near")
    start(0, "turn", OWN)
    loads[2].wait()
    cast(0, GATE, 1)
    loads[3].wait()
    cast(1, UP, 1)
    start(1, "near")
    loads[4].wait()
    cast(2, DOWN, 0)
    cast(2, DOWN, 1)

    loads[5].wait()
    loads[6].wait()
    lane = lax.broadcasted_iota(jnp.int32, (1, 512), 1)
    block = [expert_ref[i] for i in range(4)]
    of_slot = jnp.where(
        lane < 128,
        block[0],
        jnp.where(lane < 256, block[1], jnp.where(lane < 384, block[2], block[3])),
    )
    amount = slot_gate_ref[...].astype(jnp.float32) / 16.0
    for e in range(2):
        amount_e = jnp.where(of_slot == e, amount, 0.0)

        @pl.loop(0, TOK // 64)
        def _(i):
            first = pl.multiple_of(i * 64, 64)
            token = lax.broadcasted_iota(jnp.int32, (64, 512), 0) + first
            hit = jnp.where(token == slot_token_ref[...], amount_e, 0.0)
            scale_ref[e, pl.ds(first, 64), :] = jnp.sum(hit, axis=1, keepdims=True)

    row = lax.broadcasted_iota(jnp.int32, (COLS, COLS), 0)
    col = lax.broadcasted_iota(jnp.int32, (COLS, COLS), 1)
    source = ((col >> 5) & 3) * ROWS + (col >> 7) * GROUP + (col & 31)
    perm[...] = jnp.where(row == source, 1.0, 0.0).astype(jnp.bfloat16)

    arrive(0, "near")
    start(0, "near2")
    start(0, "turn", NEAR)
    arrive(0, "turn", OWN)
    start(0, "turn2", OWN)
    arrive(1, "near")
    start(1, "near2")
    for g in range(GROUPS):
        start(2 + g, "near")
    arrive(0, "near2")
    start(0, "turn", FAR)
    start(0, "core", steps=(0,))
    loads[7].wait()

    @pl.loop(0, NZ)
    def _(b):
        block = cotangent_ref[:, pl.ds(pl.multiple_of(b * COLS, COLS), COLS)]
        block = dot(block, perm[...], NN).astype(jnp.bfloat16)
        cols = pl.ds(pl.multiple_of(b * GCOLS, GCOLS), GCOLS)
        for g in range(GROUPS):
            turned[g, :, cols] = block[:, g * GCOLS : (g + 1) * GCOLS]

    for e in range(2):
        for g in range(GROUPS):

            @pl.loop(0, TOK // 32)
            def _(i):
                rows = pl.ds(pl.multiple_of(i * 32, 32), 32)
                value = turned[g, rows, :].astype(jnp.float32) * scale_ref[e, rows, :]
                d_out[e, g, rows, :] = value.astype(jnp.bfloat16)

    loads[8].wait()

    def all_y(g):
        @pl.loop(0, NX)
        def _(n):
            total = 0.0
            for e in range(2):
                rows = w_all[4 + e, n // 2, n % 2, :, :, :, pl.ds(g * GROUP, GROUP), :]
                total = total + dot(hidden[e], rows.reshape(2 * GCOLS, F), NT)
            part_y[g, 2 * n] = total[:, :GCOLS]
            part_y[g, 2 * n + 1] = total[:, GCOLS:]

    def hop(buffers, at):
        src, dst, send_sem, recv_sem = buffers
        return pltpu.make_async_remote_copy(
            src_ref=src.at[at],
            dst_ref=dst.at[at],
            send_sem=send_sem.at[at],
            recv_sem=recv_sem.at[at],
            device_id=right if at[-3] == 0 else left,
            device_id_type=MESH,
        )

    def far_first(d, h, parts):
        return (h < parts // 2) == (d == 0)

    def pieces_at(parts, step):
        order = []
        for n in range(parts):
            for d in range(2):
                h = (n + parts // 2) % parts if d == 0 else n
                if step > 0 or far_first(d, h, parts):
                    order.append((d, h))
        if step == 0:
            order = [(d, h) for h in range(parts) for d in range(2) if far_first(d, h, parts)]
        return order

    def ring(buffers, own, lead, parts, step):
        size = TOK // parts
        for d, h in pieces_at(parts, step):
            gap = HOPS - step
            b = lax.rem(z + gap, NZ) if d == 0 else lax.rem(z + NZ - gap, NZ)
            value = own[b, h * size : (h + 1) * size, :]
            if step > 1 or (step == 1 and far_first(d, h, parts)):
                before = lead + (d, h, step - 1)
                hop(buffers, before).wait_recv()
                value = value + buffers[1][before].astype(jnp.float32)
            at = lead + (d, h, step)
            buffers[0][at] = value.astype(jnp.bfloat16)
            hop(buffers, at).start()

    def collect(buffers, own, lead, parts, h):
        size = TOK // parts
        value = own[z, h * size : (h + 1) * size, :]
        for d in range(2):
            at = lead + (d, h, HOPS - 1)
            hop(buffers, at).wait_recv()
            value = value + buffers[1][at].astype(jnp.float32)
        return value.astype(jnp.bfloat16)

    def release(buffers, lead, parts):
        for step in range(HOPS):
            for d, h in pieces_at(parts, step):
                hop(buffers, lead + (d, h, step)).wait_send()

    y_buffers = (y_send, y_recv, ys_sem, yr_sem)
    x_buffers = (x_send, x_recv, xs_sem, xr_sem)

    def ring_y(g, step):
        ring(y_buffers, part_y.at[g], (g,), Y_PARTS, step)

    def end_y(g):
        size = TOK // Y_PARTS
        for h in range(Y_PARTS):
            rows = collect(y_buffers, part_y.at[g], (g,), Y_PARTS, h)
            y_rows[h * size : (h + 1) * size, g * GCOLS : (g + 1) * GCOLS] = rows

    def ring_x(step):
        ring(x_buffers, part_x, (), X_PARTS, step)

    def end_x():
        size = TOK // X_PARTS
        for n in range(X_PARTS):
            h = n // 2 + (n % 2) * (X_PARTS // 2)
            rows = collect(x_buffers, part_x, (), X_PARTS, h)
            out_ref[1, h * size : (h + 1) * size, :] = rows

    def weight_block(p, b):
        rows = w_all[p, b // 4, (b // 2) % 2, b % 2, :, :, :, :]
        return rows.reshape(COLS, F)

    def compute_dx(gap):
        @pl.loop(0, 1 if gap in (0, HOPS) else 2)
        def _(i):
            b = lax.rem(jnp.where(i == 0, z + gap, z + NZ - gap), NZ)
            total = dot(d_pre[0], weight_block(GATE[0], b), NT)
            total = total + dot(d_up[0], weight_block(UP[0], b), NT)
            total = total + dot(d_pre[1], weight_block(GATE[1], b), NT)
            part_x[b] = total + dot(d_up[1], weight_block(UP[1], b), NT)

    arrive(0, "turn", NEAR)
    start(0, "turn2", NEAR)
    for g in range(GROUPS):
        arrive(2 + g, "near")
        start(2 + g, "near2")
    arrive(1, "near2")
    arrive(0, "turn", FAR)
    start(0, "turn2", FAR)
    start(1, "turn", LOW)
    start(1, "turn", HIGH)
    start(1, "core", steps=(0,))
    start(0, "core", steps=(3, 1))
    for part in (OWN, NEAR, FAR):
        arrive(0, "turn2", part)
    start(0, "core", steps=(2,))
    for g in range(GROUPS):
        arrive(2 + g, "near2")
    arrive(0, "core", steps=(0, 3, 1, 2))
    forward(0)
    make_hidden(0)
    arrive(1, "turn", LOW)
    start(1, "turn2", LOW)
    arrive(1, "turn", HIGH)
    start(1, "turn2", HIGH)
    start(1, "core", steps=(3, 1))
    start(2, "turn")
    start(3, "turn")
    for g in range(GROUPS):
        start(2 + g, "core", steps=(0,))
    arrive(1, "turn2", LOW)
    arrive(1, "turn2", HIGH)
    start(1, "core", steps=(2,))
    arrive(2, "turn")
    start(2, "turn2")
    start(4, "turn")
    start(2, "core", steps=(3, 1))
    arrive(1, "core", steps=(0, 3, 1, 2))
    forward(2)
    make_hidden(1)
    arrive(3, "turn")
    start(3, "turn2")
    start(3, "core", steps=(3, 1))
    arrive(2, "turn2")
    start(2, "core", steps=(2,))
    arrive(2, "core", steps=(0, 3, 1, 2))
    all_y(0)
    ring_y(0, 0)
    arrive(4, "turn")
    start(4, "turn2")
    start(4, "core", steps=(3, 1))
    add_d_hidden(0)
    ring_y(0, 1)
    arrive(3, "turn2")
    start(3, "core", steps=(2,))
    arrive(3, "core", steps=(0, 3, 1, 2))
    all_y(1)
    ring_y(1, 0)
    arrive(4, "turn2")
    start(4, "core", steps=(2,))
    ring_y(0, 2)
    add_d_hidden(1)
    ring_y(1, 1)
    arrive(4, "core", steps=(0, 3, 1, 2))
    add_d_hidden(2)
    ring_y(0, 3)
    make_d()
    ring_y(1, 2)
    compute_dx(4)
    ring_x(0)
    compute_dx(3)
    ring_x(1)
    ring_y(1, 3)
    all_y(2)
    ring_y(2, 0)
    compute_dx(2)
    ring_x(2)
    ring_y(2, 1)
    end_y(0)
    compute_dx(1)
    ring_x(3)
    ring_y(2, 2)
    end_y(1)
    compute_dx(0)
    ring_y(2, 3)
    end_x()
    end_y(2)
    out_ref[0] = dot(y_rows[...], perm[...], NT).astype(jnp.bfloat16)

    for pair in range(len(PAIRS)):
        for i in range(2):
            for kind in PAIRS[pair][3]:
                copy(leg(pair, i, kind)[0], partner, pair, i, kind).wait_send()
    for g in range(GROUPS):
        release(y_buffers, (g,), Y_PARTS)
    release(x_buffers, (), X_PARTS)


def shards(tokens, cotangent, w_gate, w_up, w_down, slot_token, slot_gate, block_expert):
    vmem = pl.BlockSpec(memory_space=pltpu.VMEM)
    smem = pl.BlockSpec(memory_space=pltpu.SMEM)
    hbm = pl.BlockSpec(memory_space=pl.ANY)
    wide = (2, TOK, F)
    low, full, dma = jnp.bfloat16, jnp.float32, pltpu.SemaphoreType.DMA
    y_ring = (GROUPS, 2, Y_PARTS, HOPS)
    x_ring = (2, X_PARTS, HOPS)
    out = pl.pallas_call(
        kernel,
        out_shape=jax.ShapeDtypeStruct((2, TOK, COLS), low),
        in_specs=[smem] + [hbm] * 7,
        out_specs=vmem,
        scratch_shapes=[
            pltpu.VMEM((1, 512), jnp.int32),
            pltpu.VMEM((1, 512), jnp.int32),
            pltpu.VMEM((TOK, D), low),
            pltpu.VMEM((TOK, D), low),
            pltpu.VMEM((3, 2, ROWS, F), full),
            pltpu.VMEM((6, 2, 2, 2, 2, NC, ROWS, F), low),
            pltpu.VMEM((COLS, COLS), low),
            pltpu.VMEM((GROUPS, TOK, GK), low),
            pltpu.VMEM((2, GROUPS, TOK, GK), low),
            pltpu.VMEM((2, TOK, 1), full),
            pltpu.VMEM((4, TOK, F), full),
            pltpu.VMEM(wide, full),
            pltpu.VMEM(wide, low),
            pltpu.VMEM(wide, low),
            pltpu.VMEM(wide, low),
            pltpu.VMEM((GROUPS, NZ, TOK, GCOLS), full),
            pltpu.VMEM((NZ, TOK, COLS), full),
            pltpu.VMEM((TOK, COLS), low),
            pltpu.VMEM(y_ring + (TOK // Y_PARTS, GCOLS), low),
            pltpu.VMEM(y_ring + (TOK // Y_PARTS, GCOLS), low),
            pltpu.VMEM(x_ring + (TOK // X_PARTS, COLS), low),
            pltpu.VMEM(x_ring + (TOK // X_PARTS, COLS), low),
            dma((COPIES,)),
            dma((COPIES,)),
            dma(y_ring),
            dma(y_ring),
            dma(x_ring),
            dma(x_ring),
            dma((9,)),
        ],
        compiler_params=pltpu.CompilerParams(
            collective_id=0, has_side_effects=True, vmem_limit_bytes=63 * 1024 * 1024
        ),
    )(
        block_expert,
        slot_token.reshape(1, -1),
        slot_gate.reshape(1, -1),
        tokens,
        cotangent,
        w_gate,
        w_up,
        jnp.swapaxes(w_down, 1, 2),
    )
    return out[0], out[1]


def solution(mesh):
    in_specs = (
        P("dp", None),
        P("dp", None),
        P(None, "dp", "etp"),
        P(None, "dp", "etp"),
        P(None, "etp", "dp"),
        P("dp"),
        P("dp"),
        P("dp"),
    )
    out_specs = (P("dp", "etp"), P("dp", "etp"))
    return jax.shard_map(shards, mesh=mesh, in_specs=in_specs, out_specs=out_specs, check_vma=False)
```

```python
import functools

import jax
import jax.numpy as jnp
from jax import lax
from jax.experimental import pallas as pl
from jax.experimental.pallas import tpu as pltpu
from jax.sharding import PartitionSpec as P

MESH = pl.DeviceIdType.MESH
NX, NY, NC, NZ = 4, 4, 2, 8
ROWS = 96
HALF = ROWS // 2
D = NX * NY * NC * ROWS
F = 768
TOK = 256
COLS = D // NZ
GROUPS = 3
GROUP = ROWS // GROUPS
GCOLS = COLS // GROUPS
GK = D // GROUPS
ALL, LOW, HIGH, OWN, NEAR, FAR = range(6)


def kinds_of(parts):
    kinds = [(name, ALL, sign) for name in ("near", "near2") for sign in (1, 3)]
    kinds += [(name, part, sign) for name in ("turn", "turn2") for part in parts for sign in (1, 3)]
    return kinds + [("core", ALL, step) for step in (0, 3, 1, 2)]


PAIRS = (
    ((0, 1), 0, ROWS, kinds_of((OWN, NEAR, FAR))),
    ((2, 3), 0, ROWS, kinds_of((LOW, HIGH))),
    ((4, 5), 0, GROUP, kinds_of((ALL,))),
    ((4, 5), GROUP, GROUP, kinds_of((ALL,))),
    ((4, 5), 2 * GROUP, GROUP, kinds_of((ALL,))),
)
FIRST = [2 * sum(len(pair[3]) for pair in PAIRS[:n]) for n in range(len(PAIRS) + 1)]
COPIES = FIRST[-1]
HOPS = NZ // 2
X_PARTS = 4
Y_PARTS = 2
NT = (((1,), (1,)), ((), ()))
NN = (((1,), (0,)), ((), ()))
GATE, UP, DOWN = (0, 2), (1, 3), (4, 5)


def dot(a, b, dims):
    return lax.dot_general(a, b, dims, preferred_element_type=jnp.float32)


def kernel(
    expert_ref,
    slot_token_hbm,
    slot_gate_hbm,
    tokens_hbm,
    cotangent_hbm,
    w_gate_hbm,
    w_up_hbm,
    w_down_hbm,
    out_ref,
    slot_token_ref,
    slot_gate_ref,
    tokens_ref,
    cotangent_ref,
    masters,
    w_all,
    perm,
    turned,
    d_out,
    scale_ref,
    pre,
    d_hidden,
    hidden,
    d_pre,
    d_up,
    part_y,
    part_x,
    y_rows,
    y_send,
    y_recv,
    x_send,
    x_recv,
    g_send,
    g_recv,
    ys_sem,
    yr_sem,
    xs_sem,
    xr_sem,
    l_sem,
):
    dp = lax.axis_index("dp")
    z = lax.axis_index("etp")
    x, y, c = dp // 8, (dp // 2) % 4, dp % 2

    def dev(xx, yy, cc, zz):
        return ((xx % NX) * 8 + (yy % NY) * 2 + cc, zz % NZ)

    right, left = dev(x, y, c, z + 1), dev(x, y, c, z + NZ - 1)
    partner = dev(x, y, 1 - c, z)

    barrier = pltpu.get_barrier_semaphore()
    greeted = (
        dev(x + 1, y, c, z),
        dev(x + 3, y, c, z),
        dev(x, y + 1, c, z),
        dev(x, y + 3, c, z),
        partner,
        right,
        left,
    )
    for peer in greeted:
        pl.semaphore_signal(barrier, inc=1, device_id=peer, device_id_type=MESH)

    loads = []
    for src, dst in (
        (w_gate_hbm.at[0], masters.at[0, 0]),
        (w_up_hbm.at[0], masters.at[1, 0]),
        (w_gate_hbm.at[1], masters.at[0, 1]),
        (w_up_hbm.at[1], masters.at[1, 1]),
        (w_down_hbm, masters.at[2]),
        (slot_token_hbm, slot_token_ref),
        (slot_gate_hbm, slot_gate_ref),
        (cotangent_hbm, cotangent_ref),
        (tokens_hbm, tokens_ref),
    ):
        loads.append(pltpu.make_async_copy(src, dst, l_sem.at[len(loads)]))
        loads[-1].start()

    def cast(m, name, e):
        w_all[name[e], x // 2, x % 2, y // 2, y % 2, c, :, :] = masters[m, e].astype(jnp.bfloat16)

    def barrier_wait():
        pl.semaphore_wait(barrier, len(greeted))

    whole = slice(None)

    def slot(u):
        return (u % 4) // 2, u % 2

    def leg(pair, i, kind):
        name, part, step = kind
        m, r0, size, _ = PAIRS[pair]
        half = size // 2
        u, v = (x, y) if i == 0 else (y, x)
        back = 4 - step
        first = half if step == 3 else 0
        us = {
            ALL: (whole, whole),
            LOW: (0, whole),
            HIGH: (1, whole),
            OWN: slot(u),
            NEAR: (whole, (u + 1) % 2),
            FAR: slot(u + 2),
        }[part]

        def at(uu, vv, start=0, count=size, cc=c):
            where = uu + vv if i == 0 else vv + uu
            return w_all.at[(m[i],) + where + (cc, pl.ds(r0 + start, count), whole)]

        def peer(du, dv):
            return dev(x + du, y + dv, c, z) if i == 0 else dev(x + dv, y + du, c, z)

        if name == "near":
            return at(slot(u), slot(v)), peer(step, 0), at(slot(u + back), slot(v))
        if name == "near2":
            mine = at(slot(u + back), slot(v), first, half)
            return mine, peer(step, 0), at(slot(u + 2), slot(v), first, half)
        if name == "turn":
            return at(us, slot(v)), peer(0, step), at(us, slot(v + back))
        if name == "turn2":
            mine = at(us, slot(v + back), first, half)
            return mine, peer(0, step), at(us, slot(v + 2), first, half)
        return at(us, slot(v + step)), partner, at(us, slot(v + step), cc=1 - c)

    def copy(ref, peer, pair, i, kind):
        kinds = PAIRS[pair][3]
        at = FIRST[pair] + i * len(kinds) + kinds.index(kind)
        return pltpu.make_async_remote_copy(
            src_ref=ref,
            dst_ref=ref,
            send_sem=g_send.at[at],
            recv_sem=g_recv.at[at],
            device_id=peer,
            device_id_type=MESH,
        )

    def start(pair, name, part=ALL, steps=(1, 3)):
        for step in steps:
            for i in range(2):
                ref, peer, _ = leg(pair, i, (name, part, step))
                copy(ref, peer, pair, i, (name, part, step)).start()

    def arrive(pair, name, part=ALL, steps=(1, 3)):
        for step in steps:
            for i in range(2):
                copy(leg(pair, i, (name, part, step))[2], partner, pair, i, (name, part, step)).wait_recv()

    def forward(first):
        @pl.loop(0, 2 * (F // 256))
        def _(j):
            m = first + j // (F // 256)
            cols = pl.ds(pl.multiple_of((j % (F // 256)) * 256, 256), 256)
            rhs = w_all[m, :, :, :, :, :, :, cols].reshape(D, 256)
            pre[m, :, cols] = dot(tokens_ref[...], rhs, NN)

    def add_d_hidden(g):
        @pl.loop(0, 2 * (F // 256))
        def _(j):
            e = j // (F // 256)
            cols = pl.ds(pl.multiple_of((j % (F // 256)) * 256, 256), 256)
            rhs = w_all[4 + e, :, :, :, :, :, pl.ds(g * GROUP, GROUP), cols].reshape(GK, 256)
            total = dot(d_out[e, g], rhs, NN)
            if g > 0:
                total = total + d_hidden[e, :, cols]
            d_hidden[e, :, cols] = total

    def make_hidden(e):
        @pl.loop(0, TOK // 32)
        def _(i):
            rows = pl.ds(pl.multiple_of(i * 32, 32), 32)
            gate = pre[2 * e, rows, :]
            squash = 1.0 / (1.0 + jnp.exp(-gate))
            h = gate * squash * pre[2 * e + 1, rows, :] * scale_ref[e, rows, :]
            hidden[e, rows, :] = h.astype(jnp.bfloat16)

    def make_d():
        g = GROUPS - 1

        @pl.loop(0, 2 * (F // 256))
        def _(j):
            e = j // (F // 256)
            cols = pl.ds(pl.multiple_of((j % (F // 256)) * 256, 256), 256)
            rhs = w_all[4 + e, :, :, :, :, :, pl.ds(g * GROUP, GROUP), cols].reshape(GK, 256)
            dh = d_hidden[e, :, cols] + dot(d_out[e, g], rhs, NN)
            gate = pre[2 * e, :, cols]
            squash = 1.0 / (1.0 + jnp.exp(-gate))
            before = dh * pre[2 * e + 1, :, cols] * squash * (1.0 + gate * (1.0 - squash))
            d_pre[e, :, cols] = before.astype(jnp.bfloat16)
            d_up[e, :, cols] = (dh * (gate * squash)).astype(jnp.bfloat16)

    loads[0].wait()
    cast(0, GATE, 0)
    loads[1].wait()
    cast(1, UP, 0)
    barrier_wait()
    start(0, "near")
    start(0, "turn", OWN)
    loads[2].wait()
    cast(0, GATE, 1)
    loads[3].wait()
    cast(1, UP, 1)
    start(1, "near")
    loads[4].wait()
    cast(2, DOWN, 0)
    cast(2, DOWN, 1)

    loads[5].wait()
    loads[6].wait()
    lane = lax.broadcasted_iota(jnp.int32, (1, 512), 1)
    block = [expert_ref[i] for i in range(4)]
    of_slot = jnp.where(
        lane < 128,
        block[0],
        jnp.where(lane < 256, block[1], jnp.where(lane < 384, block[2], block[3])),
    )
    amount = slot_gate_ref[...].astype(jnp.float32) / 16.0
    for e in range(2):
        amount_e = jnp.where(of_slot == e, amount, 0.0)

        @pl.loop(0, TOK // 64)
        def _(i):
            first = pl.multiple_of(i * 64, 64)
            token = lax.broadcasted_iota(jnp.int32, (64, 512), 0) + first
            hit = jnp.where(token == slot_token_ref[...], amount_e, 0.0)
            scale_ref[e, pl.ds(first, 64), :] = jnp.sum(hit, axis=1, keepdims=True)

    row = lax.broadcasted_iota(jnp.int32, (COLS, COLS), 0)
    col = lax.broadcasted_iota(jnp.int32, (COLS, COLS), 1)
    source = ((col >> 5) & 3) * ROWS + (col >> 7) * GROUP + (col & 31)
    perm[...] = jnp.where(row == source, 1.0, 0.0).astype(jnp.bfloat16)

    arrive(0, "near")
    start(0, "near2")
    start(0, "turn", NEAR)
    arrive(0, "turn", OWN)
    start(0, "turn2", OWN)
    arrive(1, "near")
    start(1, "near2")
    for g in range(GROUPS):
        start(2 + g, "near")
    arrive(0, "near2")
    start(0, "turn", FAR)
    start(0, "core", steps=(0,))
    loads[7].wait()

    @pl.loop(0, NZ)
    def _(b):
        block = cotangent_ref[:, pl.ds(pl.multiple_of(b * COLS, COLS), COLS)]
        block = dot(block, perm[...], NN).astype(jnp.bfloat16)
        cols = pl.ds(pl.multiple_of(b * GCOLS, GCOLS), GCOLS)
        for g in range(GROUPS):
            turned[g, :, cols] = block[:, g * GCOLS : (g + 1) * GCOLS]

    for e in range(2):
        for g in range(GROUPS):

            @pl.loop(0, TOK // 32)
            def _(i):
                rows = pl.ds(pl.multiple_of(i * 32, 32), 32)
                value = turned[g, rows, :].astype(jnp.float32) * scale_ref[e, rows, :]
                d_out[e, g, rows, :] = value.astype(jnp.bfloat16)

    loads[8].wait()

    def some_y(g, first, last):
        @pl.loop(first, last)
        def _(j):
            n = lax.rem((z + HOPS) // 2 + j, NX)
            total = 0.0
            for e in range(2):
                rows = w_all[4 + e, n // 2, n % 2, :, :, :, pl.ds(g * GROUP, GROUP), :]
                total = total + dot(hidden[e], rows.reshape(2 * GCOLS, F), NT)
            part_y[g, 2 * n] = total[:, :GCOLS]
            part_y[g, 2 * n + 1] = total[:, GCOLS:]

    def hop(buffers, at):
        src, dst, send_sem, recv_sem = buffers
        return pltpu.make_async_remote_copy(
            src_ref=src.at[at],
            dst_ref=dst.at[at],
            send_sem=send_sem.at[at],
            recv_sem=recv_sem.at[at],
            device_id=right if at[-3] == 0 else left,
            device_id_type=MESH,
        )

    def far_first(d, h, parts):
        return (h < parts // 2) == (d == 0)

    def pieces_at(parts, step):
        order = []
        for n in range(parts):
            for d in range(2):
                h = (n + parts // 2) % parts if d == 0 else n
                if step > 0 or far_first(d, h, parts):
                    order.append((d, h))
        if step == 0:
            order = [(d, h) for h in range(parts) for d in range(2) if far_first(d, h, parts)]
        return order

    def ring(buffers, own, lead, parts, step):
        size = TOK // parts
        for d, h in pieces_at(parts, step):
            gap = HOPS - step
            b = lax.rem(z + gap, NZ) if d == 0 else lax.rem(z + NZ - gap, NZ)
            value = own[b, h * size : (h + 1) * size, :]
            if step > 1 or (step == 1 and far_first(d, h, parts)):
                before = lead + (d, h, step - 1)
                hop(buffers, before).wait_recv()
                value = value + buffers[1][before].astype(jnp.float32)
            at = lead + (d, h, step)
            buffers[0][at] = value.astype(jnp.bfloat16)
            hop(buffers, at).start()

    def collect(buffers, own, lead, parts, h):
        size = TOK // parts
        value = own[z, h * size : (h + 1) * size, :]
        for d in range(2):
            at = lead + (d, h, HOPS - 1)
            hop(buffers, at).wait_recv()
            value = value + buffers[1][at].astype(jnp.float32)
        return value.astype(jnp.bfloat16)

    def release(buffers, lead, parts):
        for step in range(HOPS):
            for d, h in pieces_at(parts, step):
                hop(buffers, lead + (d, h, step)).wait_send()

    y_buffers = (y_send, y_recv, ys_sem, yr_sem)
    x_buffers = (x_send, x_recv, xs_sem, xr_sem)

    def ring_y(g, step):
        ring(y_buffers, part_y.at[g], (g,), Y_PARTS, step)

    def end_y(g):
        size = TOK // Y_PARTS
        for h in range(Y_PARTS):
            rows = collect(y_buffers, part_y.at[g], (g,), Y_PARTS, h)
            y_rows[h * size : (h + 1) * size, g * GCOLS : (g + 1) * GCOLS] = rows

    def ring_x(step):
        ring(x_buffers, part_x, (), X_PARTS, step)

    def end_x():
        size = TOK // X_PARTS
        for n in range(X_PARTS):
            h = n // 2 + (n % 2) * (X_PARTS // 2)
            rows = collect(x_buffers, part_x, (), X_PARTS, h)
            out_ref[1, h * size : (h + 1) * size, :] = rows

    def weight_block(p, b):
        rows = w_all[p, b // 4, (b // 2) % 2, b % 2, :, :, :, :]
        return rows.reshape(COLS, F)

    def compute_dx(gap):
        @pl.loop(0, 1 if gap in (0, HOPS) else 2)
        def _(i):
            b = lax.rem(jnp.where(i == 0, z + gap, z + NZ - gap), NZ)
            total = dot(d_pre[0], weight_block(GATE[0], b), NT)
            total = total + dot(d_up[0], weight_block(UP[0], b), NT)
            total = total + dot(d_pre[1], weight_block(GATE[1], b), NT)
            part_x[b] = total + dot(d_up[1], weight_block(UP[1], b), NT)

    arrive(0, "turn", NEAR)
    start(0, "turn2", NEAR)
    for g in range(GROUPS):
        arrive(2 + g, "near")
        start(2 + g, "near2")
    arrive(1, "near2")
    arrive(0, "turn", FAR)
    start(0, "turn2", FAR)
    start(1, "turn", LOW)
    start(1, "turn", HIGH)
    start(1, "core", steps=(0,))
    start(0, "core", steps=(3, 1))
    for part in (OWN, NEAR, FAR):
        arrive(0, "turn2", part)
    start(0, "core", steps=(2,))
    for g in range(GROUPS):
        arrive(2 + g, "near2")
    arrive(0, "core", steps=(0, 3, 1, 2))
    forward(0)
    make_hidden(0)
    arrive(1, "turn", LOW)
    start(1, "turn2", LOW)
    arrive(1, "turn", HIGH)
    start(1, "turn2", HIGH)
    start(1, "core", steps=(3, 1))
    start(2, "turn")
    start(3, "turn")
    for g in range(GROUPS):
        start(2 + g, "core", steps=(0,))
    arrive(1, "turn2", LOW)
    arrive(1, "turn2", HIGH)
    start(1, "core", steps=(2,))
    arrive(2, "turn")
    start(2, "turn2")
    start(4, "turn")
    start(2, "core", steps=(3, 1))
    arrive(1, "core", steps=(0, 3, 1, 2))
    forward(2)
    make_hidden(1)
    arrive(3, "turn")
    start(3, "turn2")
    start(3, "core", steps=(3, 1))
    arrive(2, "turn2")
    start(2, "core", steps=(2,))
    arrive(2, "core", steps=(0, 3, 1, 2))
    some_y(0, 0, NX)
    ring_y(0, 0)
    add_d_hidden(0)
    arrive(4, "turn")
    start(4, "turn2")
    start(4, "core", steps=(3, 1))
    ring_y(0, 1)
    arrive(3, "turn2")
    start(3, "core", steps=(2,))
    arrive(3, "core", steps=(0, 3, 1, 2))
    some_y(1, 0, NX)
    ring_y(1, 0)
    ring_y(0, 2)
    arrive(4, "turn2")
    start(4, "core", steps=(2,))
    add_d_hidden(1)
    ring_y(1, 1)
    arrive(4, "core", steps=(0, 3, 1, 2))
    some_y(2, 0, 1)
    ring_y(2, 0)
    ring_y(0, 3)
    make_d()
    ring_y(1, 2)
    compute_dx(4)
    ring_x(0)
    some_y(2, 1, NX)
    ring_y(2, 1)
    compute_dx(3)
    ring_x(1)
    ring_y(1, 3)
    ring_y(2, 2)
    compute_dx(2)
    ring_x(2)
    ring_y(2, 3)
    compute_dx(1)
    ring_x(3)
    compute_dx(0)
    for g in range(GROUPS):
        end_y(g)
    out_ref[0] = dot(y_rows[...], perm[...], NT).astype(jnp.bfloat16)
    end_x()

    for pair in range(len(PAIRS)):
        for i in range(2):
            for kind in PAIRS[pair][3]:
                copy(leg(pair, i, kind)[0], partner, pair, i, kind).wait_send()
    for g in range(GROUPS):
        release(y_buffers, (g,), Y_PARTS)
    release(x_buffers, (), X_PARTS)


def shards(tokens, cotangent, w_gate, w_up, w_down, slot_token, slot_gate, block_expert):
    vmem = pl.BlockSpec(memory_space=pltpu.VMEM)
    smem = pl.BlockSpec(memory_space=pltpu.SMEM)
    hbm = pl.BlockSpec(memory_space=pl.ANY)
    wide = (2, TOK, F)
    low, full, dma = jnp.bfloat16, jnp.float32, pltpu.SemaphoreType.DMA
    y_ring = (GROUPS, 2, Y_PARTS, HOPS)
    x_ring = (2, X_PARTS, HOPS)
    out = pl.pallas_call(
        kernel,
        out_shape=jax.ShapeDtypeStruct((2, TOK, COLS), low),
        in_specs=[smem] + [hbm] * 7,
        out_specs=vmem,
        scratch_shapes=[
            pltpu.VMEM((1, 512), jnp.int32),
            pltpu.VMEM((1, 512), jnp.int32),
            pltpu.VMEM((TOK, D), low),
            pltpu.VMEM((TOK, D), low),
            pltpu.VMEM((3, 2, ROWS, F), full),
            pltpu.VMEM((6, 2, 2, 2, 2, NC, ROWS, F), low),
            pltpu.VMEM((COLS, COLS), low),
            pltpu.VMEM((GROUPS, TOK, GK), low),
            pltpu.VMEM((2, GROUPS, TOK, GK), low),
            pltpu.VMEM((2, TOK, 1), full),
            pltpu.VMEM((4, TOK, F), full),
            pltpu.VMEM(wide, full),
            pltpu.VMEM(wide, low),
            pltpu.VMEM(wide, low),
            pltpu.VMEM(wide, low),
            pltpu.VMEM((GROUPS, NZ, TOK, GCOLS), full),
            pltpu.VMEM((NZ, TOK, COLS), full),
            pltpu.VMEM((TOK, COLS), low),
            pltpu.VMEM(y_ring + (TOK // Y_PARTS, GCOLS), low),
            pltpu.VMEM(y_ring + (TOK // Y_PARTS, GCOLS), low),
            pltpu.VMEM(x_ring + (TOK // X_PARTS, COLS), low),
            pltpu.VMEM(x_ring + (TOK // X_PARTS, COLS), low),
            dma((COPIES,)),
            dma((COPIES,)),
            dma(y_ring),
            dma(y_ring),
            dma(x_ring),
            dma(x_ring),
            dma((9,)),
        ],
        compiler_params=pltpu.CompilerParams(
            collective_id=0, has_side_effects=True, vmem_limit_bytes=63 * 1024 * 1024
        ),
    )(
        block_expert,
        slot_token.reshape(1, -1),
        slot_gate.reshape(1, -1),
        tokens,
        cotangent,
        w_gate,
        w_up,
        jnp.swapaxes(w_down, 1, 2),
    )
    return out[0], out[1]


def solution(mesh):
    in_specs = (
        P("dp", None),
        P("dp", None),
        P(None, "dp", "etp"),
        P(None, "dp", "etp"),
        P(None, "etp", "dp"),
        P("dp"),
        P("dp"),
        P("dp"),
    )
    out_specs = (P("dp", "etp"), P("dp", "etp"))
    return jax.shard_map(shards, mesh=mesh, in_specs=in_specs, out_specs=out_specs, check_vma=False)
```

```python
import functools

import jax
import jax.numpy as jnp
from jax import lax
from jax.experimental import pallas as pl
from jax.experimental.pallas import tpu as pltpu
from jax.sharding import PartitionSpec as P

MESH = pl.DeviceIdType.MESH
NX, NY, NC, NZ = 4, 4, 2, 8
ROWS = 96
HALF = ROWS // 2
D = NX * NY * NC * ROWS
F = 768
TOK = 256
COLS = D // NZ
GROUPS = 3
GROUP = ROWS // GROUPS
GCOLS = COLS // GROUPS
GK = D // GROUPS
ALL, LOW, HIGH, OWN, NEAR, FAR = range(6)


def kinds_of(parts):
    kinds = [(name, ALL, sign) for name in ("near", "near2") for sign in (1, 3)]
    kinds += [(name, part, sign) for name in ("turn", "turn2") for part in parts for sign in (1, 3)]
    return kinds + [("core", ALL, step) for step in (0, 3, 1, 2)]


PAIRS = (
    ((0, 1), 0, ROWS, kinds_of((OWN, NEAR, FAR))),
    ((2, 3), 0, ROWS, kinds_of((LOW, HIGH))),
    ((4, 5), 0, GROUP, kinds_of((ALL,))),
    ((4, 5), GROUP, GROUP, kinds_of((ALL,))),
    ((4, 5), 2 * GROUP, GROUP, kinds_of((ALL,))),
)
FIRST = [2 * sum(len(pair[3]) for pair in PAIRS[:n]) for n in range(len(PAIRS) + 1)]
COPIES = FIRST[-1]
HOPS = NZ // 2
X_PARTS = 4
Y_PARTS = 2
NT = (((1,), (1,)), ((), ()))
NN = (((1,), (0,)), ((), ()))
GATE, UP, DOWN = (0, 2), (1, 3), (4, 5)


def dot(a, b, dims):
    return lax.dot_general(a, b, dims, preferred_element_type=jnp.float32)


def kernel(
    expert_ref,
    slot_token_hbm,
    slot_gate_hbm,
    tokens_hbm,
    cotangent_hbm,
    w_gate_hbm,
    w_up_hbm,
    w_down_hbm,
    out_hbm,
    out_ref,
    slot_token_ref,
    slot_gate_ref,
    tokens_ref,
    cotangent_ref,
    masters,
    w_all,
    perm,
    turned,
    d_out,
    scale_ref,
    pre,
    d_hidden,
    hidden,
    d_pre,
    d_up,
    part_y,
    part_x,
    y_rows,
    y_send,
    y_recv,
    x_send,
    x_recv,
    g_send,
    g_recv,
    ys_sem,
    yr_sem,
    xs_sem,
    xr_sem,
    l_sem,
    o_sem,
):
    dp = lax.axis_index("dp")
    z = lax.axis_index("etp")
    x, y, c = dp // 8, (dp // 2) % 4, dp % 2

    def dev(xx, yy, cc, zz):
        return ((xx % NX) * 8 + (yy % NY) * 2 + cc, zz % NZ)

    right, left = dev(x, y, c, z + 1), dev(x, y, c, z + NZ - 1)
    partner = dev(x, y, 1 - c, z)

    barrier = pltpu.get_barrier_semaphore()
    greeted = (
        dev(x + 1, y, c, z),
        dev(x + 3, y, c, z),
        dev(x, y + 1, c, z),
        dev(x, y + 3, c, z),
        partner,
        right,
        left,
    )
    for peer in greeted:
        pl.semaphore_signal(barrier, inc=1, device_id=peer, device_id_type=MESH)

    loads = []
    for src, dst in (
        (w_gate_hbm.at[0], masters.at[0, 0]),
        (w_up_hbm.at[0], masters.at[1, 0]),
        (w_gate_hbm.at[1], masters.at[0, 1]),
        (w_up_hbm.at[1], masters.at[1, 1]),
        (w_down_hbm, masters.at[2]),
        (slot_token_hbm, slot_token_ref),
        (slot_gate_hbm, slot_gate_ref),
        (cotangent_hbm, cotangent_ref),
        (tokens_hbm, tokens_ref),
    ):
        loads.append(pltpu.make_async_copy(src, dst, l_sem.at[len(loads)]))

    for load in loads[:5]:
        load.start()

    def cast(m, name, e):
        w_all[name[e], x // 2, x % 2, y // 2, y % 2, c, :, :] = masters[m, e].astype(jnp.bfloat16)

    def barrier_wait():
        pl.semaphore_wait(barrier, len(greeted))

    whole = slice(None)

    def slot(u):
        return (u % 4) // 2, u % 2

    def leg(pair, i, kind):
        name, part, step = kind
        m, r0, size, _ = PAIRS[pair]
        half = size // 2
        u, v = (x, y) if i == 0 else (y, x)
        back = 4 - step
        first = half if step == 3 else 0
        us = {
            ALL: (whole, whole),
            LOW: (0, whole),
            HIGH: (1, whole),
            OWN: slot(u),
            NEAR: (whole, (u + 1) % 2),
            FAR: slot(u + 2),
        }[part]

        def at(uu, vv, start=0, count=size, cc=c):
            where = uu + vv if i == 0 else vv + uu
            return w_all.at[(m[i],) + where + (cc, pl.ds(r0 + start, count), whole)]

        def peer(du, dv):
            return dev(x + du, y + dv, c, z) if i == 0 else dev(x + dv, y + du, c, z)

        if name == "near":
            return at(slot(u), slot(v)), peer(step, 0), at(slot(u + back), slot(v))
        if name == "near2":
            mine = at(slot(u + back), slot(v), first, half)
            return mine, peer(step, 0), at(slot(u + 2), slot(v), first, half)
        if name == "turn":
            return at(us, slot(v)), peer(0, step), at(us, slot(v + back))
        if name == "turn2":
            mine = at(us, slot(v + back), first, half)
            return mine, peer(0, step), at(us, slot(v + 2), first, half)
        return at(us, slot(v + step)), partner, at(us, slot(v + step), cc=1 - c)

    def copy(ref, peer, pair, i, kind):
        kinds = PAIRS[pair][3]
        at = FIRST[pair] + i * len(kinds) + kinds.index(kind)
        return pltpu.make_async_remote_copy(
            src_ref=ref,
            dst_ref=ref,
            send_sem=g_send.at[at],
            recv_sem=g_recv.at[at],
            device_id=peer,
            device_id_type=MESH,
        )

    def start(pair, name, part=ALL, steps=(1, 3)):
        for step in steps:
            for i in range(2):
                ref, peer, _ = leg(pair, i, (name, part, step))
                copy(ref, peer, pair, i, (name, part, step)).start()

    def arrive(pair, name, part=ALL, steps=(1, 3)):
        for step in steps:
            for i in range(2):
                copy(leg(pair, i, (name, part, step))[2], partner, pair, i, (name, part, step)).wait_recv()

    def retire(pair):
        for i in range(2):
            for kind in PAIRS[pair][3]:
                copy(leg(pair, i, kind)[0], partner, pair, i, kind).wait_send()

    def forward(first):
        @pl.loop(0, 2 * (F // 256))
        def _(j):
            m = first + j // (F // 256)
            cols = pl.ds(pl.multiple_of((j % (F // 256)) * 256, 256), 256)
            rhs = w_all[m, :, :, :, :, :, :, cols].reshape(D, 256)
            pre[m, :, cols] = dot(tokens_ref[...], rhs, NN)

    def add_d_hidden(g):
        @pl.loop(0, 2 * (F // 256))
        def _(j):
            e = j // (F // 256)
            cols = pl.ds(pl.multiple_of((j % (F // 256)) * 256, 256), 256)
            rhs = w_all[4 + e, :, :, :, :, :, pl.ds(g * GROUP, GROUP), cols].reshape(GK, 256)
            total = dot(d_out[e, g], rhs, NN)
            if g > 0:
                total = total + d_hidden[e, :, cols]
            d_hidden[e, :, cols] = total

    def make_hidden(e):
        @pl.loop(0, TOK // 32)
        def _(i):
            rows = pl.ds(pl.multiple_of(i * 32, 32), 32)
            gate = pre[2 * e, rows, :]
            squash = 1.0 / (1.0 + jnp.exp(-gate))
            h = gate * squash * pre[2 * e + 1, rows, :] * scale_ref[e, rows, :]
            hidden[e, rows, :] = h.astype(jnp.bfloat16)

    def make_d():
        g = GROUPS - 1

        @pl.loop(0, 2 * (F // 256))
        def _(j):
            e = j // (F // 256)
            cols = pl.ds(pl.multiple_of((j % (F // 256)) * 256, 256), 256)
            rhs = w_all[4 + e, :, :, :, :, :, pl.ds(g * GROUP, GROUP), cols].reshape(GK, 256)
            dh = d_hidden[e, :, cols] + dot(d_out[e, g], rhs, NN)
            gate = pre[2 * e, :, cols]
            squash = 1.0 / (1.0 + jnp.exp(-gate))
            before = dh * pre[2 * e + 1, :, cols] * squash * (1.0 + gate * (1.0 - squash))
            d_pre[e, :, cols] = before.astype(jnp.bfloat16)
            d_up[e, :, cols] = (dh * (gate * squash)).astype(jnp.bfloat16)

    loads[0].wait()
    cast(0, GATE, 0)
    loads[1].wait()
    cast(1, UP, 0)
    barrier_wait()
    start(0, "near")
    start(0, "turn", OWN)
    for load in loads[5:]:
        load.start()
    loads[2].wait()
    cast(0, GATE, 1)
    loads[3].wait()
    cast(1, UP, 1)
    start(1, "near")
    loads[4].wait()
    cast(2, DOWN, 0)
    cast(2, DOWN, 1)

    loads[5].wait()
    loads[6].wait()
    lane = lax.broadcasted_iota(jnp.int32, (1, 512), 1)
    block = [expert_ref[i] for i in range(4)]
    of_slot = jnp.where(
        lane < 128,
        block[0],
        jnp.where(lane < 256, block[1], jnp.where(lane < 384, block[2], block[3])),
    )
    amount = slot_gate_ref[...].astype(jnp.float32) / 16.0
    for e in range(2):
        amount_e = jnp.where(of_slot == e, amount, 0.0)

        @pl.loop(0, TOK // 64)
        def _(i):
            first = pl.multiple_of(i * 64, 64)
            token = lax.broadcasted_iota(jnp.int32, (64, 512), 0) + first
            hit = jnp.where(token == slot_token_ref[...], amount_e, 0.0)
            scale_ref[e, pl.ds(first, 64), :] = jnp.sum(hit, axis=1, keepdims=True)

    row = lax.broadcasted_iota(jnp.int32, (COLS, COLS), 0)
    col = lax.broadcasted_iota(jnp.int32, (COLS, COLS), 1)
    source = ((col >> 5) & 3) * ROWS + (col >> 7) * GROUP + (col & 31)
    perm[...] = jnp.where(row == source, 1.0, 0.0).astype(jnp.bfloat16)

    arrive(0, "near")
    start(0, "near2")
    start(0, "turn", NEAR)
    arrive(0, "turn", OWN)
    start(0, "turn2", OWN)
    arrive(1, "near")
    start(1, "near2")
    for g in range(GROUPS):
        start(2 + g, "near")
    arrive(0, "near2")
    start(0, "turn", FAR)
    start(0, "core", steps=(0,))
    loads[7].wait()

    @pl.loop(0, NZ)
    def _(b):
        block = cotangent_ref[:, pl.ds(pl.multiple_of(b * COLS, COLS), COLS)]
        block = dot(block, perm[...], NN).astype(jnp.bfloat16)
        cols = pl.ds(pl.multiple_of(b * GCOLS, GCOLS), GCOLS)
        for g in range(GROUPS):
            turned[g, :, cols] = block[:, g * GCOLS : (g + 1) * GCOLS]

    for e in range(2):
        for g in range(GROUPS):

            @pl.loop(0, TOK // 32)
            def _(i):
                rows = pl.ds(pl.multiple_of(i * 32, 32), 32)
                value = turned[g, rows, :].astype(jnp.float32) * scale_ref[e, rows, :]
                d_out[e, g, rows, :] = value.astype(jnp.bfloat16)

    loads[8].wait()

    def some_y(g, first, last):
        @pl.loop(first, last)
        def _(j):
            n = lax.rem((z + HOPS) // 2 + j, NX)
            total = 0.0
            for e in range(2):
                rows = w_all[4 + e, n // 2, n % 2, :, :, :, pl.ds(g * GROUP, GROUP), :]
                total = total + dot(hidden[e], rows.reshape(2 * GCOLS, F), NT)
            part_y[g, 2 * n] = total[:, :GCOLS]
            part_y[g, 2 * n + 1] = total[:, GCOLS:]

    def hop(buffers, at):
        src, dst, send_sem, recv_sem = buffers
        return pltpu.make_async_remote_copy(
            src_ref=src.at[at],
            dst_ref=dst.at[at],
            send_sem=send_sem.at[at],
            recv_sem=recv_sem.at[at],
            device_id=right if at[-3] == 0 else left,
            device_id_type=MESH,
        )

    def far_first(d, h, parts):
        return (h < parts // 2) == (d == 0)

    def pieces_at(parts, step):
        order = []
        for n in range(parts):
            for d in range(2):
                h = (n + parts // 2) % parts if d == 0 else n
                if step > 0 or far_first(d, h, parts):
                    order.append((d, h))
        if step == 0:
            order = [(d, h) for h in range(parts) for d in range(2) if far_first(d, h, parts)]
        return order

    def ring(buffers, own, lead, parts, step):
        size = TOK // parts
        for d, h in pieces_at(parts, step):
            gap = HOPS - step
            b = lax.rem(z + gap, NZ) if d == 0 else lax.rem(z + NZ - gap, NZ)
            value = own[b, h * size : (h + 1) * size, :]
            if step > 1 or (step == 1 and far_first(d, h, parts)):
                before = lead + (d, h, step - 1)
                hop(buffers, before).wait_recv()
                value = value + buffers[1][before].astype(jnp.float32)
            at = lead + (d, h, step)
            buffers[0][at] = value.astype(jnp.bfloat16)
            hop(buffers, at).start()

    def collect(buffers, own, lead, parts, h):
        size = TOK // parts
        value = own[z, h * size : (h + 1) * size, :]
        for d in range(2):
            at = lead + (d, h, HOPS - 1)
            hop(buffers, at).wait_recv()
            value = value + buffers[1][at].astype(jnp.float32)
        return value.astype(jnp.bfloat16)

    def release(buffers, lead, parts):
        for step in range(HOPS):
            for d, h in pieces_at(parts, step):
                hop(buffers, lead + (d, h, step)).wait_send()

    y_buffers = (y_send, y_recv, ys_sem, yr_sem)
    x_buffers = (x_send, x_recv, xs_sem, xr_sem)

    def ring_y(g, step):
        ring(y_buffers, part_y.at[g], (g,), Y_PARTS, step)

    def end_y(g):
        size = TOK // Y_PARTS
        for h in range(Y_PARTS):
            rows = collect(y_buffers, part_y.at[g], (g,), Y_PARTS, h)
            y_rows[h * size : (h + 1) * size, g * GCOLS : (g + 1) * GCOLS] = rows

    def ring_x(step):
        ring(x_buffers, part_x, (), X_PARTS, step)

    def store(t, h, size):
        rows = pl.ds(h * size, size)
        return pltpu.make_async_copy(out_ref.at[t, rows], out_hbm.at[t, rows], o_sem.at[t, h])

    def end_x():
        size = TOK // X_PARTS
        for n in range(X_PARTS):
            h = n // 2 + (n % 2) * (X_PARTS // 2)
            rows = collect(x_buffers, part_x, (), X_PARTS, h)
            out_ref[1, h * size : (h + 1) * size, :] = rows
            store(1, h, size).start()
        for h in range(X_PARTS):
            store(1, h, size).wait()

    def weight_block(p, b):
        rows = w_all[p, b // 4, (b // 2) % 2, b % 2, :, :, :, :]
        return rows.reshape(COLS, F)

    def compute_dx(gap):
        @pl.loop(0, 1 if gap in (0, HOPS) else 2)
        def _(i):
            b = lax.rem(jnp.where(i == 0, z + gap, z + NZ - gap), NZ)
            total = dot(d_pre[0], weight_block(GATE[0], b), NT)
            total = total + dot(d_up[0], weight_block(UP[0], b), NT)
            total = total + dot(d_pre[1], weight_block(GATE[1], b), NT)
            part_x[b] = total + dot(d_up[1], weight_block(UP[1], b), NT)

    arrive(0, "turn", NEAR)
    start(0, "turn2", NEAR)
    for g in range(GROUPS):
        arrive(2 + g, "near")
        start(2 + g, "near2")
    arrive(1, "near2")
    arrive(0, "turn", FAR)
    start(0, "turn2", FAR)
    start(1, "turn", LOW)
    start(1, "turn", HIGH)
    start(1, "core", steps=(0,))
    start(0, "core", steps=(3, 1))
    for part in (OWN, NEAR, FAR):
        arrive(0, "turn2", part)
    start(0, "core", steps=(2,))
    for g in range(GROUPS):
        arrive(2 + g, "near2")
    arrive(0, "core", steps=(0, 3, 1, 2))
    forward(0)
    make_hidden(0)
    arrive(1, "turn", LOW)
    start(1, "turn2", LOW)
    arrive(1, "turn", HIGH)
    start(1, "turn2", HIGH)
    start(1, "core", steps=(3, 1))
    start(2, "turn")
    start(3, "turn")
    for g in range(GROUPS):
        start(2 + g, "core", steps=(0,))
    arrive(1, "turn2", LOW)
    arrive(1, "turn2", HIGH)
    start(1, "core", steps=(2,))
    arrive(2, "turn")
    start(2, "turn2")
    start(4, "turn")
    start(2, "core", steps=(3, 1))
    arrive(1, "core", steps=(0, 3, 1, 2))
    forward(2)
    make_hidden(1)
    arrive(3, "turn")
    start(3, "turn2")
    start(3, "core", steps=(3, 1))
    arrive(2, "turn2")
    start(2, "core", steps=(2,))
    arrive(2, "core", steps=(0, 3, 1, 2))
    some_y(0, 0, NX)
    ring_y(0, 0)
    add_d_hidden(0)
    arrive(4, "turn")
    start(4, "turn2")
    start(4, "core", steps=(3, 1))
    ring_y(0, 1)
    retire(0)
    arrive(3, "turn2")
    start(3, "core", steps=(2,))
    arrive(3, "core", steps=(0, 3, 1, 2))
    some_y(1, 0, NX)
    ring_y(1, 0)
    ring_y(0, 2)
    arrive(4, "turn2")
    start(4, "core", steps=(2,))
    add_d_hidden(1)
    ring_y(1, 1)
    arrive(4, "core", steps=(0, 3, 1, 2))
    some_y(2, 0, 1)
    ring_y(2, 0)
    ring_y(0, 3)
    make_d()
    ring_y(1, 2)
    compute_dx(4)
    ring_x(0)
    some_y(2, 1, NX)
    ring_y(2, 1)
    compute_dx(3)
    ring_x(1)
    ring_y(1, 3)
    ring_y(2, 2)
    compute_dx(2)
    ring_x(2)
    ring_y(2, 3)
    compute_dx(1)
    ring_x(3)
    compute_dx(0)
    for pair in range(1, len(PAIRS)):
        retire(pair)
    for g in range(GROUPS):
        end_y(g)
        release(y_buffers, (g,), Y_PARTS)
    out_ref[0] = dot(y_rows[...], perm[...], NT).astype(jnp.bfloat16)
    store(0, 0, TOK).start()
    end_x()
    store(0, 0, TOK).wait()

    release(x_buffers, (), X_PARTS)


def shards(tokens, cotangent, w_gate, w_up, w_down, slot_token, slot_gate, block_expert):
    smem = pl.BlockSpec(memory_space=pltpu.SMEM)
    hbm = pl.BlockSpec(memory_space=pl.ANY)
    wide = (2, TOK, F)
    low, full, dma = jnp.bfloat16, jnp.float32, pltpu.SemaphoreType.DMA
    y_ring = (GROUPS, 2, Y_PARTS, HOPS)
    x_ring = (2, X_PARTS, HOPS)
    out = pl.pallas_call(
        kernel,
        out_shape=jax.ShapeDtypeStruct((2, TOK, COLS), low),
        in_specs=[smem] + [hbm] * 7,
        out_specs=hbm,
        scratch_shapes=[
            pltpu.VMEM((2, TOK, COLS), low),
            pltpu.VMEM((1, 512), jnp.int32),
            pltpu.VMEM((1, 512), jnp.int32),
            pltpu.VMEM((TOK, D), low),
            pltpu.VMEM((TOK, D), low),
            pltpu.VMEM((3, 2, ROWS, F), full),
            pltpu.VMEM((6, 2, 2, 2, 2, NC, ROWS, F), low),
            pltpu.VMEM((COLS, COLS), low),
            pltpu.VMEM((GROUPS, TOK, GK), low),
            pltpu.VMEM((2, GROUPS, TOK, GK), low),
            pltpu.VMEM((2, TOK, 1), full),
            pltpu.VMEM((4, TOK, F), full),
            pltpu.VMEM(wide, full),
            pltpu.VMEM(wide, low),
            pltpu.VMEM(wide, low),
            pltpu.VMEM(wide, low),
            pltpu.VMEM((GROUPS, NZ, TOK, GCOLS), full),
            pltpu.VMEM((NZ, TOK, COLS), full),
            pltpu.VMEM((TOK, COLS), low),
            pltpu.VMEM(y_ring + (TOK // Y_PARTS, GCOLS), low),
            pltpu.VMEM(y_ring + (TOK // Y_PARTS, GCOLS), low),
            pltpu.VMEM(x_ring + (TOK // X_PARTS, COLS), low),
            pltpu.VMEM(x_ring + (TOK // X_PARTS, COLS), low),
            dma((COPIES,)),
            dma((COPIES,)),
            dma(y_ring),
            dma(y_ring),
            dma(x_ring),
            dma(x_ring),
            dma((9,)),
            dma((2, X_PARTS)),
        ],
        compiler_params=pltpu.CompilerParams(
            collective_id=0, has_side_effects=True, vmem_limit_bytes=63 * 1024 * 1024
        ),
    )(
        block_expert,
        slot_token.reshape(1, -1),
        slot_gate.reshape(1, -1),
        tokens,
        cotangent,
        w_gate,
        w_up,
        jnp.swapaxes(w_down, 1, 2),
    )
    return out[0], out[1]


def solution(mesh):
    in_specs = (
        P("dp", None),
        P("dp", None),
        P(None, "dp", "etp"),
        P(None, "dp", "etp"),
        P(None, "etp", "dp"),
        P("dp"),
        P("dp"),
        P("dp"),
    )
    out_specs = (P("dp", "etp"), P("dp", "etp"))
    return jax.shard_map(shards, mesh=mesh, in_specs=in_specs, out_specs=out_specs, check_vma=False)
```

```python
import functools

import jax
import jax.numpy as jnp
from jax import lax
from jax.experimental import pallas as pl
from jax.experimental.pallas import tpu as pltpu
from jax.sharding import PartitionSpec as P

MESH = pl.DeviceIdType.MESH
NX, NY, NC, NZ = 4, 4, 2, 8
ROWS = 96
HALF = ROWS // 2
D = NX * NY * NC * ROWS
F = 768
TOK = 256
COLS = D // NZ
GROUPS = 3
GROUP = ROWS // GROUPS
GCOLS = COLS // GROUPS
GK = D // GROUPS
ALL, LOW, HIGH, OWN, NEAR, FAR = range(6)


def kinds_of(parts):
    kinds = [(name, ALL, sign) for name in ("near", "near2") for sign in (1, 3)]
    kinds += [(name, part, sign) for name in ("turn", "turn2") for part in parts for sign in (1, 3)]
    return kinds + [("core", ALL, step) for step in (0, 3, 1, 2)]


PAIRS = (
    ((0, 1), 0, ROWS, kinds_of((OWN, NEAR, FAR))),
    ((2, 3), 0, ROWS, kinds_of((LOW, HIGH))),
    ((4, 5), 0, GROUP, kinds_of((ALL,))),
    ((4, 5), GROUP, GROUP, kinds_of((ALL,))),
    ((4, 5), 2 * GROUP, GROUP, kinds_of((ALL,))),
)
FIRST = [2 * sum(len(pair[3]) for pair in PAIRS[:n]) for n in range(len(PAIRS) + 1)]
COPIES = FIRST[-1]
HOPS = NZ // 2
X_PARTS = 4
Y_PARTS = 2
NT = (((1,), (1,)), ((), ()))
NN = (((1,), (0,)), ((), ()))
GATE, UP, DOWN = (0, 2), (1, 3), (4, 5)


def dot(a, b, dims):
    return lax.dot_general(a, b, dims, preferred_element_type=jnp.float32)


def kernel(
    expert_ref,
    slot_token_hbm,
    slot_gate_hbm,
    tokens_hbm,
    cotangent_hbm,
    w_gate_hbm,
    w_up_hbm,
    w_down_hbm,
    out_hbm,
    out_ref,
    slot_token_ref,
    slot_gate_ref,
    tokens_ref,
    cotangent_ref,
    masters,
    w_all,
    perm,
    turned,
    d_out,
    scale_ref,
    pre,
    d_hidden,
    hidden,
    d_pre,
    d_up,
    part_y,
    part_x,
    y_rows,
    y_send,
    y_recv,
    x_send,
    x_recv,
    g_send,
    g_recv,
    ys_sem,
    yr_sem,
    xs_sem,
    xr_sem,
    l_sem,
    o_sem,
):
    dp = lax.axis_index("dp")
    z = lax.axis_index("etp")
    x, y, c = dp // 8, (dp // 2) % 4, dp % 2

    def dev(xx, yy, cc, zz):
        return ((xx % NX) * 8 + (yy % NY) * 2 + cc, zz % NZ)

    right, left = dev(x, y, c, z + 1), dev(x, y, c, z + NZ - 1)
    partner = dev(x, y, 1 - c, z)

    barrier = pltpu.get_barrier_semaphore()
    greeted = (
        dev(x + 1, y, c, z),
        dev(x + 3, y, c, z),
        dev(x, y + 1, c, z),
        dev(x, y + 3, c, z),
        partner,
        right,
        left,
    )
    for peer in greeted:
        pl.semaphore_signal(barrier, inc=1, device_id=peer, device_id_type=MESH)

    loads = []
    for src, dst in (
        (w_gate_hbm.at[0], masters.at[0, 0]),
        (w_up_hbm.at[0], masters.at[1, 0]),
        (w_gate_hbm.at[1], masters.at[0, 1]),
        (w_up_hbm.at[1], masters.at[1, 1]),
        (w_down_hbm, masters.at[2]),
        (slot_token_hbm, slot_token_ref),
        (slot_gate_hbm, slot_gate_ref),
        (cotangent_hbm, cotangent_ref),
        (tokens_hbm, tokens_ref),
    ):
        loads.append(pltpu.make_async_copy(src, dst, l_sem.at[len(loads)]))

    for load in loads[:5]:
        load.start()

    def cast(m, name, e):
        w_all[name[e], x // 2, x % 2, y // 2, y % 2, c, :, :] = masters[m, e].astype(jnp.bfloat16)

    def barrier_wait():
        pl.semaphore_wait(barrier, len(greeted))

    whole = slice(None)

    def slot(u):
        return (u % 4) // 2, u % 2

    def leg(pair, i, kind):
        name, part, step = kind
        m, r0, size, _ = PAIRS[pair]
        half = size // 2
        u, v = (x, y) if i == 0 else (y, x)
        back = 4 - step
        first = half if step == 3 else 0
        us = {
            ALL: (whole, whole),
            LOW: (0, whole),
            HIGH: (1, whole),
            OWN: slot(u),
            NEAR: (whole, (u + 1) % 2),
            FAR: slot(u + 2),
        }[part]

        def at(uu, vv, start=0, count=size, cc=c):
            where = uu + vv if i == 0 else vv + uu
            return w_all.at[(m[i],) + where + (cc, pl.ds(r0 + start, count), whole)]

        def peer(du, dv):
            return dev(x + du, y + dv, c, z) if i == 0 else dev(x + dv, y + du, c, z)

        if name == "near":
            return at(slot(u), slot(v)), peer(step, 0), at(slot(u + back), slot(v))
        if name == "near2":
            mine = at(slot(u + back), slot(v), first, half)
            return mine, peer(step, 0), at(slot(u + 2), slot(v), first, half)
        if name == "turn":
            return at(us, slot(v)), peer(0, step), at(us, slot(v + back))
        if name == "turn2":
            mine = at(us, slot(v + back), first, half)
            return mine, peer(0, step), at(us, slot(v + 2), first, half)
        return at(us, slot(v + step)), partner, at(us, slot(v + step), cc=1 - c)

    def copy(ref, peer, pair, i, kind):
        kinds = PAIRS[pair][3]
        at = FIRST[pair] + i * len(kinds) + kinds.index(kind)
        return pltpu.make_async_remote_copy(
            src_ref=ref,
            dst_ref=ref,
            send_sem=g_send.at[at],
            recv_sem=g_recv.at[at],
            device_id=peer,
            device_id_type=MESH,
        )

    def start(pair, name, part=ALL, steps=(1, 3), which=(0, 1)):
        for step in steps:
            for i in which:
                ref, peer, _ = leg(pair, i, (name, part, step))
                copy(ref, peer, pair, i, (name, part, step)).start()

    def arrive(pair, name, part=ALL, steps=(1, 3)):
        for step in steps:
            for i in range(2):
                copy(leg(pair, i, (name, part, step))[2], partner, pair, i, (name, part, step)).wait_recv()

    def retire(pair):
        for i in range(2):
            for kind in PAIRS[pair][3]:
                copy(leg(pair, i, kind)[0], partner, pair, i, kind).wait_send()

    def forward(first):
        @pl.loop(0, 2 * (F // 256))
        def _(j):
            m = first + j // (F // 256)
            cols = pl.ds(pl.multiple_of((j % (F // 256)) * 256, 256), 256)
            rhs = w_all[m, :, :, :, :, :, :, cols].reshape(D, 256)
            pre[m, :, cols] = dot(tokens_ref[...], rhs, NN)

    def add_d_hidden(g):
        @pl.loop(0, 2 * (F // 256))
        def _(j):
            e = j // (F // 256)
            cols = pl.ds(pl.multiple_of((j % (F // 256)) * 256, 256), 256)
            rhs = w_all[4 + e, :, :, :, :, :, pl.ds(g * GROUP, GROUP), cols].reshape(GK, 256)
            total = dot(d_out[e, g], rhs, NN)
            if g > 0:
                total = total + d_hidden[e, :, cols]
            d_hidden[e, :, cols] = total

    def make_hidden(e):
        @pl.loop(0, TOK // 32)
        def _(i):
            rows = pl.ds(pl.multiple_of(i * 32, 32), 32)
            gate = pre[2 * e, rows, :]
            squash = 1.0 / (1.0 + jnp.exp(-gate))
            h = gate * squash * pre[2 * e + 1, rows, :] * scale_ref[e, rows, :]
            hidden[e, rows, :] = h.astype(jnp.bfloat16)

    def make_d():
        g = GROUPS - 1

        @pl.loop(0, 2 * (F // 256))
        def _(j):
            e = j // (F // 256)
            cols = pl.ds(pl.multiple_of((j % (F // 256)) * 256, 256), 256)
            rhs = w_all[4 + e, :, :, :, :, :, pl.ds(g * GROUP, GROUP), cols].reshape(GK, 256)
            dh = d_hidden[e, :, cols] + dot(d_out[e, g], rhs, NN)
            gate = pre[2 * e, :, cols]
            squash = 1.0 / (1.0 + jnp.exp(-gate))
            before = dh * pre[2 * e + 1, :, cols] * squash * (1.0 + gate * (1.0 - squash))
            d_pre[e, :, cols] = before.astype(jnp.bfloat16)
            d_up[e, :, cols] = (dh * (gate * squash)).astype(jnp.bfloat16)

    loads[0].wait()
    cast(0, GATE, 0)
    barrier_wait()
    start(0, "near", which=(0,))
    start(0, "turn", OWN, which=(0,))
    loads[1].wait()
    cast(1, UP, 0)
    start(0, "near", which=(1,))
    start(0, "turn", OWN, which=(1,))
    for load in loads[5:]:
        load.start()
    loads[2].wait()
    cast(0, GATE, 1)
    loads[3].wait()
    cast(1, UP, 1)
    start(1, "near")
    loads[4].wait()
    cast(2, DOWN, 0)
    cast(2, DOWN, 1)

    loads[5].wait()
    loads[6].wait()
    lane = lax.broadcasted_iota(jnp.int32, (1, 512), 1)
    block = [expert_ref[i] for i in range(4)]
    of_slot = jnp.where(
        lane < 128,
        block[0],
        jnp.where(lane < 256, block[1], jnp.where(lane < 384, block[2], block[3])),
    )
    amount = slot_gate_ref[...].astype(jnp.float32) / 16.0
    for e in range(2):
        amount_e = jnp.where(of_slot == e, amount, 0.0)

        @pl.loop(0, TOK // 64)
        def _(i):
            first = pl.multiple_of(i * 64, 64)
            token = lax.broadcasted_iota(jnp.int32, (64, 512), 0) + first
            hit = jnp.where(token == slot_token_ref[...], amount_e, 0.0)
            scale_ref[e, pl.ds(first, 64), :] = jnp.sum(hit, axis=1, keepdims=True)

    row = lax.broadcasted_iota(jnp.int32, (COLS, COLS), 0)
    col = lax.broadcasted_iota(jnp.int32, (COLS, COLS), 1)
    source = ((col >> 5) & 3) * ROWS + (col >> 7) * GROUP + (col & 31)
    perm[...] = jnp.where(row == source, 1.0, 0.0).astype(jnp.bfloat16)

    arrive(0, "near")
    start(0, "near2")
    start(0, "turn", NEAR)
    arrive(0, "turn", OWN)
    start(0, "turn2", OWN)
    arrive(1, "near")
    start(1, "near2")
    for g in range(GROUPS):
        start(2 + g, "near")
    arrive(0, "near2")
    start(0, "turn", FAR)
    start(0, "core", steps=(0,))
    loads[7].wait()

    @pl.loop(0, NZ)
    def _(b):
        block = cotangent_ref[:, pl.ds(pl.multiple_of(b * COLS, COLS), COLS)]
        block = dot(block, perm[...], NN).astype(jnp.bfloat16)
        cols = pl.ds(pl.multiple_of(b * GCOLS, GCOLS), GCOLS)
        for g in range(GROUPS):
            turned[g, :, cols] = block[:, g * GCOLS : (g + 1) * GCOLS]

    for e in range(2):
        for g in range(GROUPS):

            @pl.loop(0, TOK // 32)
            def _(i):
                rows = pl.ds(pl.multiple_of(i * 32, 32), 32)
                value = turned[g, rows, :].astype(jnp.float32) * scale_ref[e, rows, :]
                d_out[e, g, rows, :] = value.astype(jnp.bfloat16)

    loads[8].wait()

    def some_y(g, first, last):
        @pl.loop(first, last)
        def _(j):
            n = lax.rem((z + HOPS) // 2 + j, NX)
            total = 0.0
            for e in range(2):
                rows = w_all[4 + e, n // 2, n % 2, :, :, :, pl.ds(g * GROUP, GROUP), :]
                total = total + dot(hidden[e], rows.reshape(2 * GCOLS, F), NT)
            part_y[g, 2 * n] = total[:, :GCOLS]
            part_y[g, 2 * n + 1] = total[:, GCOLS:]

    def hop(buffers, at):
        src, dst, send_sem, recv_sem = buffers
        return pltpu.make_async_remote_copy(
            src_ref=src.at[at],
            dst_ref=dst.at[at],
            send_sem=send_sem.at[at],
            recv_sem=recv_sem.at[at],
            device_id=right if at[-3] == 0 else left,
            device_id_type=MESH,
        )

    def far_first(d, h, parts):
        return (h < parts // 2) == (d == 0)

    def pieces_at(parts, step):
        order = []
        for n in range(parts):
            for d in range(2):
                h = (n + parts // 2) % parts if d == 0 else n
                if step > 0 or far_first(d, h, parts):
                    order.append((d, h))
        if step == 0:
            order = [(d, h) for h in range(parts) for d in range(2) if far_first(d, h, parts)]
        return order

    def ring(buffers, own, lead, parts, step):
        size = TOK // parts
        for d, h in pieces_at(parts, step):
            gap = HOPS - step
            b = lax.rem(z + gap, NZ) if d == 0 else lax.rem(z + NZ - gap, NZ)
            value = own[b, h * size : (h + 1) * size, :]
            if step > 1 or (step == 1 and far_first(d, h, parts)):
                before = lead + (d, h, step - 1)
                hop(buffers, before).wait_recv()
                value = value + buffers[1][before].astype(jnp.float32)
            at = lead + (d, h, step)
            buffers[0][at] = value.astype(jnp.bfloat16)
            hop(buffers, at).start()

    def collect(buffers, own, lead, parts, h):
        size = TOK // parts
        value = own[z, h * size : (h + 1) * size, :]
        for d in range(2):
            at = lead + (d, h, HOPS - 1)
            hop(buffers, at).wait_recv()
            value = value + buffers[1][at].astype(jnp.float32)
        return value.astype(jnp.bfloat16)

    def release(buffers, lead, parts):
        for step in range(HOPS):
            for d, h in pieces_at(parts, step):
                hop(buffers, lead + (d, h, step)).wait_send()

    y_buffers = (y_send, y_recv, ys_sem, yr_sem)
    x_buffers = (x_send, x_recv, xs_sem, xr_sem)

    def ring_y(g, step):
        ring(y_buffers, part_y.at[g], (g,), Y_PARTS, step)

    def end_y(g):
        size = TOK // Y_PARTS
        for h in range(Y_PARTS):
            rows = collect(y_buffers, part_y.at[g], (g,), Y_PARTS, h)
            y_rows[h * size : (h + 1) * size, g * GCOLS : (g + 1) * GCOLS] = rows

    def ring_x(step):
        ring(x_buffers, part_x, (), X_PARTS, step)

    def store(t, h, size):
        rows = pl.ds(h * size, size)
        return pltpu.make_async_copy(out_ref.at[t, rows], out_hbm.at[t, rows], o_sem.at[t, h])

    def end_x():
        size = TOK // X_PARTS
        for n in range(X_PARTS):
            h = n // 2 + (n % 2) * (X_PARTS // 2)
            rows = collect(x_buffers, part_x, (), X_PARTS, h)
            out_ref[1, h * size : (h + 1) * size, :] = rows
            store(1, h, size).start()
        for h in range(X_PARTS):
            store(1, h, size).wait()

    def weight_block(p, b):
        rows = w_all[p, b // 4, (b // 2) % 2, b % 2, :, :, :, :]
        return rows.reshape(COLS, F)

    def compute_dx(gap):
        @pl.loop(0, 1 if gap in (0, HOPS) else 2)
        def _(i):
            b = lax.rem(jnp.where(i == 0, z + gap, z + NZ - gap), NZ)
            total = dot(d_pre[0], weight_block(GATE[0], b), NT)
            total = total + dot(d_up[0], weight_block(UP[0], b), NT)
            total = total + dot(d_pre[1], weight_block(GATE[1], b), NT)
            part_x[b] = total + dot(d_up[1], weight_block(UP[1], b), NT)

    arrive(0, "turn", NEAR)
    start(0, "turn2", NEAR)
    for g in range(GROUPS):
        arrive(2 + g, "near")
        start(2 + g, "near2")
    arrive(1, "near2")
    arrive(0, "turn", FAR)
    start(0, "turn2", FAR)
    start(1, "turn", LOW)
    start(1, "turn", HIGH)
    start(1, "core", steps=(0,))
    start(0, "core", steps=(3, 1))
    for part in (OWN, NEAR, FAR):
        arrive(0, "turn2", part)
    start(0, "core", steps=(2,))
    for g in range(GROUPS):
        arrive(2 + g, "near2")
    arrive(0, "core", steps=(0, 3, 1, 2))
    forward(0)
    make_hidden(0)
    arrive(1, "turn", LOW)
    start(1, "turn2", LOW)
    arrive(1, "turn", HIGH)
    start(1, "turn2", HIGH)
    start(1, "core", steps=(3, 1))
    start(2, "turn")
    start(3, "turn")
    for g in range(GROUPS):
        start(2 + g, "core", steps=(0,))
    arrive(1, "turn2", LOW)
    arrive(1, "turn2", HIGH)
    start(1, "core", steps=(2,))
    arrive(2, "turn")
    start(2, "turn2")
    start(4, "turn")
    start(2, "core", steps=(3, 1))
    arrive(1, "core", steps=(0, 3, 1, 2))
    forward(2)
    make_hidden(1)
    arrive(3, "turn")
    start(3, "turn2")
    start(3, "core", steps=(3, 1))
    arrive(2, "turn2")
    start(2, "core", steps=(2,))
    arrive(2, "core", steps=(0, 3, 1, 2))
    some_y(0, 0, NX)
    ring_y(0, 0)
    add_d_hidden(0)
    arrive(4, "turn")
    start(4, "turn2")
    start(4, "core", steps=(3, 1))
    ring_y(0, 1)
    retire(0)
    arrive(3, "turn2")
    start(3, "core", steps=(2,))
    arrive(3, "core", steps=(0, 3, 1, 2))
    some_y(1, 0, NX)
    ring_y(1, 0)
    ring_y(0, 2)
    arrive(4, "turn2")
    start(4, "core", steps=(2,))
    add_d_hidden(1)
    ring_y(1, 1)
    arrive(4, "core", steps=(0, 3, 1, 2))
    some_y(2, 0, 1)
    ring_y(2, 0)
    ring_y(0, 3)
    make_d()
    ring_y(1, 2)
    compute_dx(4)
    ring_x(0)
    some_y(2, 1, NX)
    ring_y(2, 1)
    compute_dx(3)
    ring_x(1)
    ring_y(1, 3)
    ring_y(2, 2)
    compute_dx(2)
    ring_x(2)
    ring_y(2, 3)
    compute_dx(1)
    ring_x(3)
    compute_dx(0)
    for pair in range(1, len(PAIRS)):
        retire(pair)
    for g in range(GROUPS):
        end_y(g)
        release(y_buffers, (g,), Y_PARTS)
    out_ref[0] = dot(y_rows[...], perm[...], NT).astype(jnp.bfloat16)
    store(0, 0, TOK).start()
    end_x()
    store(0, 0, TOK).wait()

    release(x_buffers, (), X_PARTS)


def shards(tokens, cotangent, w_gate, w_up, w_down, slot_token, slot_gate, block_expert):
    smem = pl.BlockSpec(memory_space=pltpu.SMEM)
    hbm = pl.BlockSpec(memory_space=pl.ANY)
    wide = (2, TOK, F)
    low, full, dma = jnp.bfloat16, jnp.float32, pltpu.SemaphoreType.DMA
    y_ring = (GROUPS, 2, Y_PARTS, HOPS)
    x_ring = (2, X_PARTS, HOPS)
    out = pl.pallas_call(
        kernel,
        out_shape=jax.ShapeDtypeStruct((2, TOK, COLS), low),
        in_specs=[smem] + [hbm] * 7,
        out_specs=hbm,
        scratch_shapes=[
            pltpu.VMEM((2, TOK, COLS), low),
            pltpu.VMEM((1, 512), jnp.int32),
            pltpu.VMEM((1, 512), jnp.int32),
            pltpu.VMEM((TOK, D), low),
            pltpu.VMEM((TOK, D), low),
            pltpu.VMEM((3, 2, ROWS, F), full),
            pltpu.VMEM((6, 2, 2, 2, 2, NC, ROWS, F), low),
            pltpu.VMEM((COLS, COLS), low),
            pltpu.VMEM((GROUPS, TOK, GK), low),
            pltpu.VMEM((2, GROUPS, TOK, GK), low),
            pltpu.VMEM((2, TOK, 1), full),
            pltpu.VMEM((4, TOK, F), full),
            pltpu.VMEM(wide, full),
            pltpu.VMEM(wide, low),
            pltpu.VMEM(wide, low),
            pltpu.VMEM(wide, low),
            pltpu.VMEM((GROUPS, NZ, TOK, GCOLS), full),
            pltpu.VMEM((NZ, TOK, COLS), full),
            pltpu.VMEM((TOK, COLS), low),
            pltpu.VMEM(y_ring + (TOK // Y_PARTS, GCOLS), low),
            pltpu.VMEM(y_ring + (TOK // Y_PARTS, GCOLS), low),
            pltpu.VMEM(x_ring + (TOK // X_PARTS, COLS), low),
            pltpu.VMEM(x_ring + (TOK // X_PARTS, COLS), low),
            dma((COPIES,)),
            dma((COPIES,)),
            dma(y_ring),
            dma(y_ring),
            dma(x_ring),
            dma(x_ring),
            dma((9,)),
            dma((2, X_PARTS)),
        ],
        compiler_params=pltpu.CompilerParams(
            collective_id=0, has_side_effects=True, vmem_limit_bytes=63 * 1024 * 1024
        ),
    )(
        block_expert,
        slot_token.reshape(1, -1),
        slot_gate.reshape(1, -1),
        tokens,
        cotangent,
        w_gate,
        w_up,
        jnp.swapaxes(w_down, 1, 2),
    )
    return out[0], out[1]


def solution(mesh):
    in_specs = (
        P("dp", None),
        P("dp", None),
        P(None, "dp", "etp"),
        P(None, "dp", "etp"),
        P(None, "etp", "dp"),
        P("dp"),
        P("dp"),
        P("dp"),
    )
    out_specs = (P("dp", "etp"), P("dp", "etp"))
    return jax.shard_map(shards, mesh=mesh, in_specs=in_specs, out_specs=out_specs, check_vma=False)
```
